32 devices in a mesh: rows: 8 (over y, x, core), chan: 4 (over z).
Axes of the slice: x: 2, y: 2, z: 4, core: 2. Of those that a mesh axis runs over, the one named last changes fastest.
Arguments:
- features: bfloat16 [1024, 1, 4096], P('chan', None, 'rows'), may hold values from -24 to 24
- gain_first: float32 [1024], P('chan'), may hold values from 0.1 to 1.9
- weight_first: bfloat16 [3, 3, 3, 1024, 1024], P(None, None, None, 'chan'), may hold values from -0.0390625 to 0.0390625
- bias_first: float32 [1024], P('chan'), may hold values from -3 to 3
- gain_second: float32 [1024], P('chan'), may hold values from 0.1 to 1.9
- weight_second: bfloat16 [3, 3, 3, 1024, 1024], P(None, None, None, 'chan'), may hold values from -0.0390625 to 0.0390625
- bias_second: float32 [1024], P('chan'), may hold values from -3 to 3
Outputs:
- block_out: bfloat16 [1024, 1, 4096], P('chan', None, 'rows')
The draws below stay inside these ranges and needn't reach their ends.
All inputs are finite; a program needn't handle non-finite values.
Results may differ from the reference program's by a relative error of at most 0.0022.
Values may be sent and summed in bfloat16 or wider, within the bound.
No kernel may reach another device: no remote copies, remote signals or barrier semaphores. Data moves between devices by JAX's collectives and lax.ppermute only.
A program may use at most 64 MiB of HBM per device.

```python
import jax
import jax.numpy as jnp
from jax import lax

CH = 1024
FRAMES = 1
WIDTH = 64
HEIGHT = 64


def draw_features(key, part):
    first_key, second_key = jax.random.split(jax.random.fold_in(key, 11), 2)
    channel_scale = jnp.exp(jnp.log(3.0) * jnp.arange(CH, dtype=jnp.float32) / CH)[:, None, None]
    cell_scale = jnp.exp(jax.random.uniform(second_key, (1, FRAMES, HEIGHT * WIDTH), jnp.float32, -0.69, 0.69))
    base = jnp.clip(jax.random.normal(first_key, (CH, FRAMES, HEIGHT * WIDTH), jnp.float32), -4.0, 4.0)
    return (base * channel_scale * cell_scale).astype(jnp.bfloat16)


def steps_of(rng, extent, shards, smallest, high):
    level = 1.0
    for dim, blocks in shards:
        draws = jax.random.uniform(jax.random.fold_in(jax.random.fold_in(rng, 6), dim), (blocks,), jnp.float32, smallest / len(shards), high / len(shards))
        level = level * jnp.repeat(jnp.exp(draws), extent[dim] // blocks).reshape((-1,) + (1,) * (len(extent) - 1 - dim))
    return level


def centred(key, dims, deviation, limit, cuts=(), kind=jnp.bfloat16):
    level = steps_of(key, dims, cuts, -0.22, 0.18) if cuts else 1.0
    entries = jax.random.normal(key, dims, jnp.float32) * deviation * level
    return jnp.minimum(jnp.maximum(entries, -limit), limit).astype(kind)


def setup_inputs(seed: int = 0) -> dict:
    splits = jax.random.split(jax.random.key(seed), 8)
    return {
        "features": draw_features(jax.random.fold_in(splits[7], 71), 0),
        "gain_first": jnp.clip(1.0 + 0.18 * jax.random.normal(splits[1], (CH,), jnp.float32), 0.1, 1.9),
        "weight_first": centred(splits[2], (3, 3, 3, CH, CH), (27 * CH) ** -0.5, 0.0390625, ((3, 4),)),
        "bias_first": centred(splits[3], (CH,), 0.5, 3.0, ((0, 4),), jnp.float32),
        "gain_second": jnp.clip(1.0 + 0.18 * jax.random.normal(splits[4], (CH,), jnp.float32), 0.1, 1.9),
        "weight_second": centred(splits[5], (3, 3, 3, CH, CH), (27 * CH) ** -0.5, 0.0390625, ((3, 4),)),
        "bias_second": centred(splits[6], (CH,), 0.5, 3.0, ((0, 4),), jnp.float32),
    }


def activate(values, gain):
    mean_sq = lax.optimization_barrier(jnp.mean(values * values, axis=0, keepdims=True))
    return jax.nn.silu(values * gain[:, None, None] / jnp.sqrt(mean_sq + 1e-06)).astype(jnp.bfloat16)

def convolve(data, kernel):
    channels, frames, cells = data.shape
    grid = data.reshape(1, channels, frames, HEIGHT, WIDTH)
    result = lax.conv_general_dilated(grid, kernel, (1, 1, 1), ((2, 0), (1, 1), (1, 1)), dimension_numbers=('NCDHW', 'DHWOI', 'NCDHW'), preferred_element_type=jnp.float32)
    return result[0].astype(jnp.float32).reshape(kernel.shape[3], frames, cells)

def reference(features, gain_first, weight_first, bias_first, gain_second, weight_second, bias_second):
    source = features.astype(jnp.float32)
    first = activate(source, gain_first)
    middle = convolve(first, weight_first) + bias_first[:, None, None]
    second = activate(middle, gain_second)
    return (source + convolve(second, weight_second) + bias_second[:, None, None]).astype(jnp.bfloat16)
```

```python
import jax
import jax.numpy as jnp
from jax import lax
from jax.experimental import pallas as pl
from jax.experimental.pallas import tpu as pltpu
from jax.sharding import PartitionSpec as P

WIDTH = 64
LANES = 128


def shift_along(block, axis, step):
    count = lax.axis_size(axis)
    pairs = [(i, i + step) for i in range(count) if 0 <= i + step < count]
    return lax.ppermute(block, axis, pairs)


def ring(block, axis, step=1):
    count = lax.axis_size(axis)
    return lax.ppermute(block, axis, [(i, (i + step) % count) for i in range(count)])


def ring_gather(block, axis):
    blocks = [block]
    for _ in range(lax.axis_size(axis) - 1):
        blocks.append(ring(blocks[-1], axis))
    return blocks


def conv_kernel(count, frame, residual, *refs):
    place = refs[0]
    edges = refs[1 : 1 + count]
    inner = refs[1 + count : 1 + 2 * count]
    above, above_last, below, below_last, gains, bias, weights = refs[1 + 2 * count : 8 + 2 * count]
    rest = refs[8 + 2 * count :]
    if residual:
        source, out, taps, acts, sums, sems = rest
    else:
        out, taps, acts, sums, sems = rest
    copies = [
        pltpu.make_async_copy(weights.at[frame, q, s], taps.at[q * 3 + s], sems.at[q * 3 + s])
        for q in range(3)
        for s in range(3)
    ]
    for copy in copies:
        copy.start()
    width = edges[0].shape[1]
    cells = acts.shape[1] - 2 * WIDTH
    total = acts.shape[2]

    def parts(r):
        top = above[r] if r < count - 1 else above_last[...]
        low = below[r] if r < count - 1 else below_last[...]
        return jnp.concatenate(
            [top, edges[r][:WIDTH], inner[r][...], edges[r][WIDTH:], low], axis=0
        ).astype(jnp.float32)

    squares = jnp.zeros((cells + 2 * WIDTH, 1), jnp.float32)
    for r in range(count):
        values = parts(r)
        squares += jnp.sum(values * values, axis=1, keepdims=True)
    sums[...] = lax.rsqrt(squares / total + 1e-6)
    column = lax.broadcasted_iota(jnp.int32, (cells + 2 * WIDTH, width), 0) % WIDTH
    for r in range(count):
        owner = lax.rem(place[0] + count - r, count)
        lanes = pl.ds(pl.multiple_of(owner * width, width), width)
        scaled = parts(r) * gains[r : r + 1, :] * sums[...]
        value = scaled / (1.0 + jnp.exp(-scaled))
        acts[1, :, lanes] = value.astype(jnp.bfloat16)
        before = jnp.where(column == 0, 0.0, pltpu.roll(value, 1, 0))
        acts[0, :, lanes] = before.astype(jnp.bfloat16)
        after = jnp.where(column == WIDTH - 1, 0.0, pltpu.roll(value, value.shape[0] - 1, 0))
        acts[2, :, lanes] = after.astype(jnp.bfloat16)
    result = jnp.broadcast_to(bias[...], (cells, bias.shape[1]))
    for q in range(3):
        for s in range(3):
            copies[q * 3 + s].wait()
            result += lax.dot_general(
                acts[s, q * WIDTH : q * WIDTH + cells, :],
                taps[q * 3 + s],
                (((1,), (1,)), ((), ())),
                preferred_element_type=jnp.float32,
            )
    if residual:
        result = result + source[...].astype(jnp.float32)
        out[...] = result.T.astype(out.dtype)
    else:
        out[...] = result.astype(out.dtype)


def conv_stage(block, gains, bias, weights, source=None):
    count = lax.axis_size("chan")
    cells, width = block.shape
    edges = ring_gather(jnp.concatenate([block[:WIDTH], block[cells - WIDTH :]], axis=0), "chan")
    inner = ring_gather(block[WIDTH : cells - WIDTH], "chan")
    above = shift_along(jnp.stack([e[WIDTH:] for e in edges[:-1]]), "rows", 1)
    below = shift_along(jnp.stack([e[:WIDTH] for e in edges[:-1]]), "rows", -1)
    above_last = shift_along(edges[-1][WIDTH:], "rows", 1)
    below_last = shift_along(edges[-1][:WIDTH], "rows", -1)
    outs = weights.shape[3]
    operands = [
        lax.axis_index("chan").astype(jnp.int32).reshape(1),
        *edges,
        *inner,
        above,
        above_last,
        below,
        below_last,
        gains,
        bias.reshape(1, outs),
        weights,
    ]
    if source is not None:
        operands.append(source)
    vmem = pl.BlockSpec(memory_space=pltpu.VMEM)
    in_specs = [pl.BlockSpec(memory_space=pltpu.SMEM)] + [vmem] * (len(operands) - 1)
    in_specs[7 + 2 * count] = pl.BlockSpec(memory_space=pl.ANY)
    total = width * count
    shape = (cells, outs) if source is None else (outs, cells)

    def kernel(*refs):
        conv_kernel(count, weights.shape[0] - 1, source is not None, *refs)

    return pl.pallas_call(
        kernel,
        out_shape=jax.ShapeDtypeStruct(shape, jnp.bfloat16),
        in_specs=in_specs,
        out_specs=vmem,
        scratch_shapes=[
            pltpu.VMEM((9, outs, total), jnp.bfloat16),
            pltpu.VMEM((3, cells + 2 * WIDTH, total), jnp.bfloat16),
            pltpu.VMEM((cells + 2 * WIDTH, 1), jnp.float32),
            pltpu.SemaphoreType.DMA((9,)),
        ],
        compiler_params=pltpu.CompilerParams(vmem_limit_bytes=40 << 20),
    )(*operands)


def padded(block, width):
    low = shift_along(block[..., block.shape[-1] - width :], "rows", 1)
    high = shift_along(block[..., :width], "rows", -1)
    return jnp.concatenate([low, block, high], axis=-1)


def activate(values, gain, total):
    mean_sq = lax.psum(jnp.sum(values * values, axis=0, keepdims=True), "chan") / total
    return jax.nn.silu(values * gain[:, None, None] / jnp.sqrt(mean_sq + 1e-06)).astype(jnp.bfloat16)


def convolve(block, kernel):
    whole = padded(lax.all_gather(block, "chan", axis=0, tiled=True), WIDTH)
    channels, frames, cells = whole.shape
    grid = whole.reshape(1, channels, frames, cells // WIDTH, WIDTH)
    result = lax.conv_general_dilated(
        grid,
        kernel,
        (1, 1, 1),
        ((2, 0), (0, 0), (1, 1)),
        dimension_numbers=("NCDHW", "DHWOI", "NCDHW"),
        preferred_element_type=jnp.float32,
    )
    return result[0].reshape(kernel.shape[3], frames, cells - 2 * WIDTH)


def general(features, gain_first, weight_first, bias_first, gain_second, weight_second, bias_second):
    total = weight_first.shape[4]
    source = features.astype(jnp.float32)
    middle = convolve(activate(source, gain_first, total), weight_first) + bias_first[:, None, None]
    result = convolve(activate(middle, gain_second, total), weight_second)
    return (source + result + bias_second[:, None, None]).astype(jnp.bfloat16)


def on_device(
    features, gain_first, weight_first, bias_first, gain_second, weight_second, bias_second
):
    channels, frames, cells = features.shape
    if frames != 1 or channels % LANES or cells < 3 * WIDTH:
        return general(
            features, gain_first, weight_first, bias_first, gain_second, weight_second, bias_second
        )
    block = features.reshape(channels, cells).T
    count = lax.axis_size("chan")
    pair = jnp.stack([gain_first, gain_second])
    pairs = jnp.stack([pair] + [ring(pair, "chan", r) for r in range(1, count)])
    middle = conv_stage(block, pairs[:, 0], bias_first, weight_first)
    out = conv_stage(middle, pairs[:, 1], bias_second, weight_second, block)
    return out.reshape(channels, frames, cells)


def solution(mesh):
    in_specs = (
        P("chan", None, "rows"),
        P("chan"),
        P(None, None, None, "chan", None),
        P("chan"),
        P("chan"),
        P(None, None, None, "chan", None),
        P("chan"),
    )
    return jax.shard_map(
        on_device, mesh=mesh, in_specs=in_specs, out_specs=P("chan", None, "rows"), check_vma=False
    )
```

```python
import jax
import jax.numpy as jnp
from jax import lax
from jax.experimental import pallas as pl
from jax.experimental.pallas import tpu as pltpu
from jax.sharding import PartitionSpec as P

WIDTH = 64
LANES = 128


def shift_along(block, axis, step):
    count = lax.axis_size(axis)
    pairs = [(i, i + step) for i in range(count) if 0 <= i + step < count]
    return lax.ppermute(block, axis, pairs)


def ring(block, axis, step=1):
    count = lax.axis_size(axis)
    return lax.ppermute(block, axis, [(i, (i + step) % count) for i in range(count)])


def column_of(row, lanes=LANES):
    return jnp.broadcast_to(row, (lanes, row.shape[1])).T[:, :1]


def row_of(column, lanes=LANES):
    return jnp.broadcast_to(column, (column.shape[0], lanes)).T[:1]


def silu(values):
    return values / (1.0 + jnp.exp(-values))


def inverse_rms(row, total):
    return 1.0 / jnp.sqrt(column_of(row) / total + 1e-6)


def conv_kernel(pieces, normed, last, total, *refs):
    place, refs = refs[0], refs[1:]
    cells_in, refs = refs[:pieces], refs[pieces:]
    if not normed:
        (gain, sums), refs = refs[:2], refs[2:]
    (taps, start), refs = refs[:2], refs[2:]
    if last == "out":
        source, refs = refs[0], refs[1:]
    outs, acts = refs[:-1], refs[-1]
    if pieces == 3:
        joined = [ref[...] for ref in cells_in]
    else:
        top, edge, body, low = cells_in
        joined = [top[...], edge[:WIDTH], body[...], edge[WIDTH:], low[...]]
    values = jnp.concatenate(joined, axis=0).astype(jnp.float32)
    if not normed:
        values = silu(values * gain[...] * inverse_rms(sums[...], total))
    length, width = values.shape
    cells = length - 2 * WIDTH
    column = lax.broadcasted_iota(jnp.int32, (length, 1), 0) % WIDTH
    acts[1] = values.astype(jnp.bfloat16)
    before = jnp.where(column == 0, 0.0, pltpu.roll(values, 1, 0))
    acts[0] = before.astype(jnp.bfloat16)
    after = jnp.where(column == WIDTH - 1, 0.0, pltpu.roll(values, length - 1, 0))
    acts[2] = after.astype(jnp.bfloat16)
    lanes = pl.ds(pl.multiple_of(place[0] * width, width), width)
    left = [acts[s, q * WIDTH : q * WIDTH + cells] for q in range(3) for s in range(3)]
    right = [taps[t, :, lanes] for t in range(9)]
    result = start[...] + lax.dot_general(
        jnp.concatenate(left, axis=1),
        jnp.concatenate(right, axis=1),
        (((1,), (1,)), ((), ())),
        preferred_element_type=jnp.float32,
    )
    if last == "out":
        outs[0][...] = (result + source[...].astype(jnp.float32)).T.astype(outs[0].dtype)
    else:
        outs[0][...] = result
    if last == "sums":
        outs[1][...] = row_of(jnp.sum(result * result, axis=1, keepdims=True))


VMEM = pl.BlockSpec(memory_space=pltpu.VMEM)
PARAMS = pltpu.CompilerParams(vmem_limit_bytes=16 << 20)


def conv_part(owner, cells_in, norm, taps, start, total, last="", source=None):
    outs, width = taps.shape[1], cells_in[0].shape[1]
    length = sum(piece.shape[0] for piece in cells_in)
    cells = length - 2 * WIDTH
    operands = [owner, *cells_in, *norm, taps, start]
    if source is not None:
        operands.append(source)
    shapes = [jax.ShapeDtypeStruct((cells, outs), jnp.float32)]
    if last == "out":
        shapes = [jax.ShapeDtypeStruct((outs, cells), jnp.bfloat16)]
    if last == "sums":
        shapes.append(jax.ShapeDtypeStruct((1, cells), jnp.float32))
    pieces, first = len(cells_in), start.shape[0] == 1

    def kernel(*refs):
        conv_kernel(pieces, not norm, last, total, *refs)

    alias = {} if first or last == "out" else {len(operands) - 1: 0}
    result = pl.pallas_call(
        kernel,
        out_shape=shapes,
        in_specs=[pl.BlockSpec(memory_space=pltpu.SMEM)] + [VMEM] * (len(operands) - 1),
        out_specs=[VMEM] * len(shapes),
        input_output_aliases=alias,
        scratch_shapes=[pltpu.VMEM((3, length, width), jnp.bfloat16)],
        compiler_params=PARAMS,
    )(*operands)
    return result if len(result) > 1 else result[0]


def fetch_kernel(frame, weights, taps, sems):
    copies = [
        pltpu.make_async_copy(weights.at[frame, q, s], taps.at[q * 3 + s], sems.at[q * 3 + s])
        for q in range(3)
        for s in range(3)
    ]
    for copy in copies:
        copy.start()
    for copy in copies:
        copy.wait()


def fetch(weights):
    outs, total = weights.shape[3:]
    return pl.pallas_call(
        lambda *refs: fetch_kernel(weights.shape[0] - 1, *refs),
        out_shape=pltpu.VMEM((9, outs, total), weights.dtype),
        in_specs=[pl.BlockSpec(memory_space=pltpu.HBM)],
        out_specs=VMEM,
        scratch_shapes=[pltpu.SemaphoreType.DMA((9,))],
        compiler_params=PARAMS,
    )(pltpu.with_memory_space_constraint(weights, pltpu.HBM))


def act_kernel(total, values, gain, sums, out):
    out[...] = silu(values[...] * gain[...] * inverse_rms(sums[...], total)).astype(out.dtype)


def act(values, gain, sums, total):
    return pl.pallas_call(
        lambda *refs: act_kernel(total, *refs),
        out_shape=jax.ShapeDtypeStruct(values.shape, jnp.bfloat16),
        in_specs=[VMEM] * 3,
        out_specs=VMEM,
        compiler_params=PARAMS,
    )(values, gain, sums)


def edges_of(block):
    return block[:WIDTH], block[block.shape[0] - WIDTH :]


def halo(top, low):
    count = lax.axis_size("rows")
    even = lax.axis_index("rows") % 2 == 0
    rounds = []
    for begin in range(2):
        pairs = [(i, i + 1) for i in range(begin, count - 1, 2)]
        send = jnp.where(even, low, top) if begin == 0 else jnp.where(even, top, low)
        rounds.append(lax.ppermute(send, "rows", pairs + [(b, a) for a, b in pairs]))
    return jnp.where(even, rounds[1], rounds[0]), jnp.where(even, rounds[0], rounds[1])


def others(value, axis):
    return [ring(value, axis, step) for step in range(1, lax.axis_size(axis))]


def conv_stage(block, groups, norms, weights, bias, total, last, source=None, halos=()):
    count = lax.axis_size("chan")
    place = lax.axis_index("chan").astype(jnp.int32)
    cells = block.shape[0]
    result = bias.reshape(1, -1)
    taps = fetch(weights)
    blocks = [block]
    for _ in range(1, count - 1):
        blocks.append(ring(blocks[-1], "chan"))
    edges = [edges_of(b) for b in blocks]
    edge = ring(jnp.concatenate(edges[-1], axis=0), "chan")
    edges.append((edge[:WIDTH], edge[WIDTH:]))
    body = ring(blocks[-1][WIDTH : cells - WIDTH], "chan")
    halos = list(halos)
    for group in groups:
        pair = halo(*[jnp.stack([edges[r][side] for r in group]) for side in range(2)])
        halos += [(pair[0][k], pair[1][k]) for k in range(len(group))]
    for r in range(count):
        up, down = halos[r]
        end = r == count - 1
        pieces = [up, edge, body, down] if end else [up, blocks[r], down]
        owner = lax.rem(place + count - r, count).reshape(1)
        result = conv_part(
            owner, pieces, norms[r], taps, result, total, last if end else "", source if end else None
        )
    return result


def groups_of(count):
    return [range(1, count)], [range(count - 2), range(count - 2, count)]


def padded(block, width):
    low = shift_along(block[..., block.shape[-1] - width :], "rows", 1)
    high = shift_along(block[..., :width], "rows", -1)
    return jnp.concatenate([low, block, high], axis=-1)


def activate(values, gain, total):
    mean_sq = lax.psum(jnp.sum(values * values, axis=0, keepdims=True), "chan") / total
    return jax.nn.silu(values * gain[:, None, None] / jnp.sqrt(mean_sq + 1e-06)).astype(jnp.bfloat16)


def convolve(block, kernel):
    whole = padded(lax.all_gather(block, "chan", axis=0, tiled=True), WIDTH)
    channels, frames, cells = whole.shape
    grid = whole.reshape(1, channels, frames, cells // WIDTH, WIDTH)
    result = lax.conv_general_dilated(
        grid,
        kernel,
        (1, 1, 1),
        ((2, 0), (0, 0), (1, 1)),
        dimension_numbers=("NCDHW", "DHWOI", "NCDHW"),
        preferred_element_type=jnp.float32,
    )
    return result[0].reshape(kernel.shape[3], frames, cells - 2 * WIDTH)


def general(features, gain_first, weight_first, bias_first, gain_second, weight_second, bias_second):
    total = weight_first.shape[4]
    source = features.astype(jnp.float32)
    middle = convolve(activate(source, gain_first, total), weight_first) + bias_first[:, None, None]
    result = convolve(activate(middle, gain_second, total), weight_second)
    return (source + result + bias_second[:, None, None]).astype(jnp.bfloat16)


def on_device(
    features, gain_first, weight_first, bias_first, gain_second, weight_second, bias_second
):
    channels, frames, cells = features.shape
    count = lax.axis_size("chan")
    if frames != 1 or channels % LANES or cells < 3 * WIDTH or count < 3:
        return general(
            features, gain_first, weight_first, bias_first, gain_second, weight_second, bias_second
        )
    out = resident(
        features, gain_first, weight_first, bias_first, gain_second, weight_second, bias_second
    )
    return out


def resident(
    features, gain_first, weight_first, bias_first, gain_second, weight_second, bias_second
):
    channels, frames, cells = features.shape
    count, total = lax.axis_size("chan"), weight_first.shape[4]
    first, then = groups_of(count)
    block = features.reshape(channels, cells).T
    own_halo = halo(*edges_of(block))
    source = jnp.concatenate([own_halo[0], block, own_halo[1]], axis=0).astype(jnp.float32)
    sums = jnp.sum(source * source, axis=1)
    note = jnp.concatenate([sums, gain_first])
    notes = [note] + others(note, "chan")
    length = sums.shape[0]
    sums = sum(note[:length] for note in notes).reshape(1, -1)
    norms = [(note[length:].reshape(1, -1), sums) for note in notes]
    middle, sums = conv_stage(
        block, first, norms, weight_first, bias_first, total, "sums", halos=[own_halo]
    )
    sums = sums + sum(others(sums, "chan"))
    second = act(middle, gain_second.reshape(1, -1), sums, total)
    out = conv_stage(second, then, [()] * count, weight_second, bias_second, total, "out", block)
    return out.reshape(channels, frames, cells)


def solution(mesh):
    in_specs = (
        P("chan", None, "rows"),
        P("chan"),
        P(None, None, None, "chan", None),
        P("chan"),
        P("chan"),
        P(None, None, None, "chan", None),
        P("chan"),
    )
    return jax.shard_map(
        on_device, mesh=mesh, in_specs=in_specs, out_specs=P("chan", None, "rows"), check_vma=False
    )
```

```python
import jax
import jax.numpy as jnp
from jax import lax
from jax.experimental import pallas as pl
from jax.experimental.pallas import tpu as pltpu
from jax.sharding import PartitionSpec as P

WIDTH = 64
LANES = 128


def shift_along(block, axis, step):
    count = lax.axis_size(axis)
    pairs = [(i, i + step) for i in range(count) if 0 <= i + step < count]
    return lax.ppermute(block, axis, pairs)


VMEM = pl.BlockSpec(memory_space=pltpu.VMEM)
HBM = pl.BlockSpec(memory_space=pltpu.HBM)
PARAMS = pltpu.CompilerParams(vmem_limit_bytes=20 << 20)


def column_of(row):
    return jnp.broadcast_to(row, (LANES, row.shape[1])).T[:, :1]


def row_of(column):
    return jnp.broadcast_to(column, (column.shape[0], LANES)).T[:1]


def silu(values):
    return values / (1.0 + jnp.exp(-values))


def filter_copies(frame, weights, taps, sems):
    return [
        pltpu.make_async_copy(weights.at[frame, q, s], taps.at[q * 3 + s], sems.at[q * 3 + s])
        for q in range(3)
        for s in range(3)
    ]


def fetch_kernel(frame, weights, taps, sems):
    copies = filter_copies(frame, weights, taps, sems)
    for copy in copies:
        copy.start()
    for copy in copies:
        copy.wait()


def fetch(weights):
    outs, total = weights.shape[3:]
    return pl.pallas_call(
        lambda *refs: fetch_kernel(weights.shape[0] - 1, *refs),
        out_shape=pltpu.VMEM((9, outs, total), weights.dtype),
        in_specs=[HBM],
        out_specs=VMEM,
        scratch_shapes=[pltpu.SemaphoreType.DMA((9,))],
        compiler_params=PARAMS,
    )(pltpu.with_memory_space_constraint(weights, pltpu.HBM))


def shifted(values):
    cells = values.shape[0]
    column = lax.broadcasted_iota(jnp.int32, (cells, 1), 0) % WIDTH
    before = jnp.where(column == 0, 0.0, pltpu.roll(values, 1, 0))
    after = jnp.where(column == WIDTH - 1, 0.0, pltpu.roll(values, cells - 1, 0))
    return [part.astype(jnp.bfloat16) for part in (before, values, after)]


def matmul(left, right):
    return lax.dot_general(
        jnp.concatenate(left, axis=1),
        jnp.concatenate(right, axis=1),
        (((1,), (1,)), ((), ())),
        preferred_element_type=jnp.float32,
    )


def steps_of(count):
    return sorted(range(1, count), key=lambda step: (step == count // 2, step != count - 1, step))


def owner_of(k):
    return lax.axis_index("chan") ^ [0, *steps_of(lax.axis_size("chan"))][k]


def lanes_of(owner, width):
    return pl.ds(pl.multiple_of(owner * width, width), width)


def main_taps(block, taps, owner, acts):
    cells, width = block.shape
    zeros = jnp.zeros((WIDTH, width), acts.dtype)
    for s, part in enumerate(shifted(block.astype(jnp.float32))):
        acts[s, :WIDTH] = zeros
        acts[s, WIDTH : WIDTH + cells] = part
        acts[s, WIDTH + cells :] = zeros
    lanes = lanes_of(owner, width)
    left = [acts[s, q * WIDTH : q * WIDTH + cells] for q in range(3) for s in range(3)]
    return matmul(left, [taps[t, :, lanes] for t in range(9)])


def edge_taps(block, taps, owner):
    cells, width = block.shape
    lanes = lanes_of(owner, width)
    above = matmul(shifted(block[:WIDTH].astype(jnp.float32)), [taps[6 + s, :, lanes] for s in range(3)])
    low = shifted(block[cells - WIDTH :].astype(jnp.float32))
    return above, matmul(low, [taps[s, :, lanes] for s in range(3)])


def send_kernel(source, note, out, gain, sems):
    width, cells = source.shape
    copies = [
        pltpu.make_async_copy(source, out.at[:width], sems.at[0]),
        pltpu.make_async_copy(note, gain, sems.at[1]),
    ]
    for copy in copies:
        copy.start()
    copies[1].wait()
    parts, rest = [], gain[...]
    for _ in range(3):
        parts.append(rest.astype(jnp.bfloat16).astype(jnp.float32))
        rest = rest - parts[-1]
    rows = jnp.concatenate([*parts, jnp.zeros((5, width), jnp.float32)], axis=0)
    if cells > width:
        rows = jnp.concatenate([rows, jnp.zeros((8, cells - width), jnp.float32)], axis=1)
    out[width:] = rows.astype(out.dtype)
    copies[0].wait()


def to_send(block, gain):
    width, cells = block.shape
    return pl.pallas_call(
        send_kernel,
        out_shape=pltpu.VMEM((width + 8, cells), block.dtype),
        in_specs=[HBM] * 2,
        out_specs=VMEM,
        scratch_shapes=[pltpu.VMEM(gain.shape, gain.dtype), pltpu.SemaphoreType.DMA((2,))],
        compiler_params=PARAMS,
    )(*[pltpu.with_memory_space_constraint(value, pltpu.HBM) for value in (block, gain)])


def first_kernel(total, count, *refs):
    blocks, (taps, out, first, second) = refs[:count], refs[count:]
    width = blocks[0].shape[0] - 8

    def block(k):
        return blocks[k][:width].astype(jnp.float32)

    squares = sum(jnp.sum(block(k) * block(k), axis=0, keepdims=True) for k in range(count))
    inverse = column_of(1.0 / jnp.sqrt(squares / total + 1e-6))
    for k in range(count):
        note = blocks[k][width:, :width].astype(jnp.float32)
        gain = (note[0:1] + note[1:2]) + note[2:3]
        out[k] = silu(block(k).T * gain * inverse).astype(out.dtype)
    parts = [edge_taps(out[k], taps, owner_of(k)) for k in range(count)]
    first[...], second[...] = to_swap(sum(p[0] for p in parts), sum(p[1] for p in parts))


def first_act(blocks, taps):
    outs, total = taps.shape[1:]
    width, cells = blocks[0].shape[0] - 8, blocks[0].shape[1]
    count = len(blocks)
    edge = jax.ShapeDtypeStruct((WIDTH, outs), jnp.float32)
    return pl.pallas_call(
        lambda *refs: first_kernel(total, count, *refs),
        out_shape=[
            jax.ShapeDtypeStruct((count, cells, width), jnp.bfloat16),
            edge,
            edge,
        ],
        in_specs=[VMEM] * (count + 1),
        out_specs=[VMEM] * 3,
        compiler_params=PARAMS,
    )(*blocks, taps)


def first_main_kernel(blocks, taps, out, acts):
    for k in range(blocks.shape[0]):
        part = main_taps(blocks[k], taps, owner_of(k), acts.at[k % 2])
        out[...] = part if k == 0 else out[...] + part


def first_main(blocks, taps):
    _, cells, width = blocks.shape
    return pl.pallas_call(
        first_main_kernel,
        out_shape=jax.ShapeDtypeStruct((cells, taps.shape[1]), jnp.float32),
        in_specs=[VMEM] * 2,
        out_specs=VMEM,
        scratch_shapes=[pltpu.VMEM((2, 3, cells + 2 * WIDTH, width), jnp.bfloat16)],
        compiler_params=PARAMS,
    )(blocks, taps)


def edge_kernel(k, block, taps, *refs):
    before, outs = refs[:-2], refs[-2:]
    parts = edge_taps(block[...], taps, owner_of(k))
    if before:
        parts = [ref[...] + part for ref, part in zip(before, parts)]
    outs[0][...], outs[1][...] = to_swap(*parts)


def main_kernel(k, block, taps, *refs):
    before, out, acts = refs[:-2], refs[-2], refs[-1]
    part = main_taps(block[...], taps, owner_of(k), acts)
    out[...] = before[0][...] + part if before else part


def both_kernel(k, block, taps, *refs):
    before, outs, acts = refs[:-4], refs[-4:-1], refs[-1]
    parts = [main_taps(block[...], taps, owner_of(k), acts), *edge_taps(block[...], taps, owner_of(k))]
    for place, part in enumerate(parts):
        outs[place][...] = before[place][...] + part if before else part


def second_part(kernel, k, block, taps, before):
    cells, width = block.shape
    sizes = {main_kernel: [cells], edge_kernel: [WIDTH] * 2, both_kernel: [cells, WIDTH, WIDTH]}[kernel]
    operands = [block, taps, *before]
    acts = pltpu.VMEM((3, cells + 2 * WIDTH, width), jnp.bfloat16)
    return pl.pallas_call(
        lambda *refs: kernel(k, *refs),
        out_shape=[jax.ShapeDtypeStruct((size, taps.shape[1]), jnp.float32) for size in sizes],
        in_specs=[VMEM] * len(operands),
        out_specs=[VMEM] * len(sizes),
        input_output_aliases={2 + i: i for i in range(len(before))},
        scratch_shapes=[] if kernel is edge_kernel else [acts],
        compiler_params=PARAMS,
    )(*operands)


def to_swap(above, below):
    even = lax.axis_index("rows") % 2 == 0
    return jnp.where(even, below, above), jnp.where(even, above, below)


def joined(main, first, second, bias):
    row = lax.axis_index("rows")
    even, top, low = row % 2 == 0, row == 0, row == lax.axis_size("rows") - 1
    above = jnp.where(even, second[...], first[...])
    below = jnp.where(even, first[...], second[...])
    above, below = jnp.where(top, 0.0, above), jnp.where(low, 0.0, below)
    end = main.shape[0] - WIDTH
    rows = [main[:WIDTH] + above, main[WIDTH:end], main[end:] + below]
    return jnp.concatenate(rows, axis=0) + bias[...]


def middle_kernel(main, first, second, bias, out, squares):
    middle = joined(main, first, second, bias)
    out[...] = middle
    squares[...] = row_of(jnp.sum(middle * middle, axis=1, keepdims=True))


def out_kernel(main, first, second, bias, source, out):
    result = joined(main, first, second, bias).T + source[...].astype(jnp.float32)
    out[...] = result.astype(out.dtype)


def act_kernel(total, values, gain, *refs):
    sums, out = refs[:-1], refs[-1]
    inverse = column_of(1.0 / jnp.sqrt(sum(ref[...] for ref in sums) / total + 1e-6))
    out[...] = silu(values[...] * gain[...] * inverse).astype(out.dtype)


def act(values, gain, sums, total):
    return pl.pallas_call(
        lambda *refs: act_kernel(total, *refs),
        out_shape=jax.ShapeDtypeStruct(values.shape, jnp.bfloat16),
        in_specs=[VMEM] * (2 + len(sums)),
        out_specs=VMEM,
        compiler_params=PARAMS,
    )(values, gain, *sums)


def with_row_neighbours(sends):
    count = lax.axis_size("rows")
    rounds = []
    for begin, send in enumerate(sends):
        pairs = [(i, (i + 1) % count) for i in range(begin, count, 2)]
        rounds.append(lax.ppermute(send, "rows", pairs + [(b, a) for a, b in pairs]))
    return rounds


def swap(value, step):
    return lax.ppermute(value, "chan", [(i, i ^ step) for i in range(lax.axis_size("chan"))])


def gathered(block):
    blocks = {0: block}
    for step in steps_of(lax.axis_size("chan")):
        blocks[step] = swap(block, step)
    return blocks


def resident(
    features, gain_first, weight_first, bias_first, gain_second, weight_second, bias_second
):
    channels, frames, cells = features.shape
    total = weight_first.shape[4]
    count = lax.axis_size("chan")
    source = features.reshape(channels, cells)
    taps = fetch(weight_first)
    blocks = gathered(to_send(source, gain_first.reshape(1, -1)))
    blocks, *edges = first_act(list(blocks.values()), taps)
    edges = with_row_neighbours(edges)
    main = first_main(blocks, taps)
    middle, squares = pl.pallas_call(
        middle_kernel,
        out_shape=[
            jax.ShapeDtypeStruct((cells, channels), jnp.float32),
            jax.ShapeDtypeStruct((1, cells), jnp.float32),
        ],
        in_specs=[VMEM] * 4,
        out_specs=[VMEM] * 2,
        compiler_params=PARAMS,
    )(main, *edges, bias_first.reshape(1, -1))
    others = [swap(squares, step) for step in range(count - 1, 0, -1)]
    block = act(middle, gain_second.reshape(1, -1), [squares, *others], total)
    taps = fetch(weight_second)
    blocks = gathered(block)
    parts = ()
    for k, step in enumerate(blocks):
        part = lambda kernel, before: second_part(kernel, k, blocks[step], taps, before)
        if k < count - 1:
            parts = part(both_kernel, parts)
    edges = part(edge_kernel, parts[1:])
    edges = with_row_neighbours(edges)
    main = part(main_kernel, parts[:1])
    out = pl.pallas_call(
        out_kernel,
        out_shape=jax.ShapeDtypeStruct((channels, cells), features.dtype),
        in_specs=[VMEM] * 5,
        out_specs=VMEM,
        compiler_params=PARAMS,
    )(main[0], *edges, bias_second.reshape(1, -1), source)
    return out.reshape(channels, frames, cells)


def padded(block, width):
    low = shift_along(block[..., block.shape[-1] - width :], "rows", 1)
    high = shift_along(block[..., :width], "rows", -1)
    return jnp.concatenate([low, block, high], axis=-1)


def activate(values, gain, total):
    mean_sq = lax.psum(jnp.sum(values * values, axis=0, keepdims=True), "chan") / total
    return jax.nn.silu(values * gain[:, None, None] / jnp.sqrt(mean_sq + 1e-06)).astype(jnp.bfloat16)


def convolve(block, kernel):
    whole = padded(lax.all_gather(block, "chan", axis=0, tiled=True), WIDTH)
    channels, frames, cells = whole.shape
    grid = whole.reshape(1, channels, frames, cells // WIDTH, WIDTH)
    result = lax.conv_general_dilated(
        grid,
        kernel,
        (1, 1, 1),
        ((2, 0), (0, 0), (1, 1)),
        dimension_numbers=("NCDHW", "DHWOI", "NCDHW"),
        preferred_element_type=jnp.float32,
    )
    return result[0].reshape(kernel.shape[3], frames, cells - 2 * WIDTH)


def general(features, gain_first, weight_first, bias_first, gain_second, weight_second, bias_second):
    total = weight_first.shape[4]
    source = features.astype(jnp.float32)
    middle = convolve(activate(source, gain_first, total), weight_first) + bias_first[:, None, None]
    result = convolve(activate(middle, gain_second, total), weight_second)
    return (source + result + bias_second[:, None, None]).astype(jnp.bfloat16)


def on_device(
    features, gain_first, weight_first, bias_first, gain_second, weight_second, bias_second
):
    channels, frames, cells = features.shape
    chan, rows = lax.axis_size("chan"), lax.axis_size("rows")
    narrow = channels % LANES or cells < 3 * WIDTH or channels > cells
    if frames != 1 or narrow or chan < 2 or chan & (chan - 1) or rows % 2:
        return general(
            features, gain_first, weight_first, bias_first, gain_second, weight_second, bias_second
        )
    out = resident(
        features, gain_first, weight_first, bias_first, gain_second, weight_second, bias_second
    )
    return out


def solution(mesh):
    in_specs = (
        P("chan", None, "rows"),
        P("chan"),
        P(None, None, None, "chan", None),
        P("chan"),
        P("chan"),
        P(None, None, None, "chan", None),
        P("chan"),
    )
    return jax.shard_map(
        on_device, mesh=mesh, in_specs=in_specs, out_specs=P("chan", None, "rows"), check_vma=False
    )
```

```python
import jax
import jax.numpy as jnp
from jax import lax
from jax.experimental import pallas as pl
from jax.experimental.pallas import tpu as pltpu
from jax.sharding import PartitionSpec as P

WIDTH = 64
LANES = 128


def shift_along(block, axis, step):
    count = lax.axis_size(axis)
    pairs = [(i, i + step) for i in range(count) if 0 <= i + step < count]
    return lax.ppermute(block, axis, pairs)


VMEM = pl.BlockSpec(memory_space=pltpu.VMEM)
HBM = pl.BlockSpec(memory_space=pltpu.HBM)
PARAMS = pltpu.CompilerParams(vmem_limit_bytes=20 << 20)


def column_of(row):
    return jnp.broadcast_to(row, (LANES, row.shape[1])).T[:, :1]


def row_of(column):
    return jnp.broadcast_to(column, (column.shape[0], LANES)).T[:1]


def silu(values):
    return values / (1.0 + jnp.exp(-values))


def filter_copies(frame, weights, taps, sems):
    return [
        pltpu.make_async_copy(weights.at[frame, q, s], taps.at[q * 3 + s], sems.at[q * 3 + s])
        for q in range(3)
        for s in range(3)
    ]


def fetch_kernel(frame, weights, taps, sems):
    copies = filter_copies(frame, weights, taps, sems)
    for copy in copies:
        copy.start()
    for copy in copies:
        copy.wait()


def fetch(weights):
    outs, total = weights.shape[3:]
    return pl.pallas_call(
        lambda *refs: fetch_kernel(weights.shape[0] - 1, *refs),
        out_shape=pltpu.VMEM((9, outs, total), weights.dtype),
        in_specs=[HBM],
        out_specs=VMEM,
        scratch_shapes=[pltpu.SemaphoreType.DMA((9,))],
        compiler_params=PARAMS,
    )(pltpu.with_memory_space_constraint(weights, pltpu.HBM))


def shifted(values):
    cells = values.shape[0]
    column = lax.broadcasted_iota(jnp.int32, (cells, 1), 0) % WIDTH
    before = jnp.where(column == 0, 0.0, pltpu.roll(values, 1, 0))
    after = jnp.where(column == WIDTH - 1, 0.0, pltpu.roll(values, cells - 1, 0))
    return [part.astype(jnp.bfloat16) for part in (before, values, after)]


def matmul(left, right):
    return lax.dot_general(
        jnp.concatenate(left, axis=1),
        jnp.concatenate(right, axis=1),
        (((1,), (1,)), ((), ())),
        preferred_element_type=jnp.float32,
    )


def steps_of(count):
    return sorted(range(1, count), key=lambda step: (step != count // 2, step))


def owner_of(k):
    return lax.axis_index("chan") ^ [0, *steps_of(lax.axis_size("chan"))][k]


def lanes_of(owner, width):
    return pl.ds(pl.multiple_of(owner * width, width), width)


def main_taps(block, taps, owner, acts):
    cells, width = block.shape
    zeros = jnp.zeros((WIDTH, width), acts.dtype)
    for s, part in enumerate(shifted(block.astype(jnp.float32))):
        acts[s, :WIDTH] = zeros
        acts[s, WIDTH : WIDTH + cells] = part
        acts[s, WIDTH + cells :] = zeros
    lanes = lanes_of(owner, width)
    left = [acts[s, q * WIDTH : q * WIDTH + cells] for q in range(3) for s in range(3)]
    return matmul(left, [taps[t, :, lanes] for t in range(9)])


def edge_taps(block, taps, owner):
    cells, width = block.shape
    lanes = lanes_of(owner, width)
    above = matmul(shifted(block[:WIDTH].astype(jnp.float32)), [taps[6 + s, :, lanes] for s in range(3)])
    low = shifted(block[cells - WIDTH :].astype(jnp.float32))
    return above, matmul(low, [taps[s, :, lanes] for s in range(3)])


def gain_rows(parts, lanes, rows):
    width = parts[0].shape[1]
    step = min(width, lanes)
    pieces = [part[:, k : k + step] for part in parts for k in range(0, width, step)]
    result = jnp.concatenate([*pieces, jnp.zeros((rows - len(pieces), step), jnp.float32)], axis=0)
    if lanes > step:
        result = jnp.concatenate([result, jnp.zeros((rows, lanes - step), jnp.float32)], axis=1)
    return result


def gain_from(note, width):
    step = min(width, note.shape[1])
    count = width // step
    rows = [note[k : k + 1, :step].astype(jnp.float32) for k in range(3 * count)]
    parts = [jnp.concatenate(rows[k * count : (k + 1) * count], axis=1) for k in range(3)]
    return (parts[0] + parts[1]) + parts[2]


def send_kernel(source, note, whole, edge, body, gain, sems):
    width, cells = source.shape
    copies = [
        pltpu.make_async_copy(source, whole.at[:width], sems.at[0]),
        pltpu.make_async_copy(note, gain, sems.at[1]),
    ]
    for copy in copies:
        copy.start()
    copies[1].wait()
    parts, rest = [], gain[...]
    for _ in range(3):
        parts.append(rest.astype(jnp.bfloat16).astype(jnp.float32))
        rest = rest - parts[-1]
    for out in (whole, edge):
        out[width:] = gain_rows(parts, out.shape[1], out.shape[0] - width).astype(out.dtype)
    copies[0].wait()
    edge[:width] = edges_in(whole[:width])
    body[...] = whole[:width, WIDTH : cells - WIDTH]


def edges_in(block):
    cells = block.shape[1]
    return jnp.concatenate([block[:, :WIDTH], block[:, cells - WIDTH :]], axis=1)


def to_send(block, gain):
    width, cells = block.shape
    pieces = 3 * pl.cdiv(width, 2 * WIDTH)
    shapes = [(width + 8, cells), (width + 8 * pl.cdiv(pieces, 8), 2 * WIDTH), (width, cells - 2 * WIDTH)]
    return pl.pallas_call(
        send_kernel,
        out_shape=[pltpu.VMEM(shape, block.dtype) for shape in shapes],
        in_specs=[HBM] * 2,
        out_specs=[VMEM] * 3,
        scratch_shapes=[pltpu.VMEM(gain.shape, gain.dtype), pltpu.SemaphoreType.DMA((2,))],
        compiler_params=PARAMS,
    )(*[pltpu.with_memory_space_constraint(value, pltpu.HBM) for value in (block, gain)])


def normed(values, gains, total):
    values = [value.astype(jnp.float32) for value in values]
    squares = sum(jnp.sum(value * value, axis=0, keepdims=True) for value in values)
    inverse = column_of(1.0 / jnp.sqrt(squares / total + 1e-6))
    return [silu(value.T * gain * inverse).astype(jnp.bfloat16) for value, gain in zip(values, gains)]


def first_gains(wholes, edge, width):
    return [gain_from(ref[width:], width) for ref in (*wholes, edge)]


def first_edge_kernel(total, *refs):
    wholes, (edge, taps, first, second) = refs[:-4], refs[-4:]
    width = wholes[0].shape[0] - 8
    values = [edges_in(ref[:width]) for ref in wholes] + [edge[:width]]
    blocks = normed(values, first_gains(wholes, edge, width), total)
    parts = [edge_taps(block, taps, owner_of(k)) for k, block in enumerate(blocks)]
    first[...], second[...] = to_swap(sum(p[0] for p in parts), sum(p[1] for p in parts))


def first_edge(wholes, edge, taps):
    outs, total = taps.shape[1:]
    return pl.pallas_call(
        lambda *refs: first_edge_kernel(total, *refs),
        out_shape=[jax.ShapeDtypeStruct((WIDTH, outs), jnp.float32)] * 2,
        in_specs=[VMEM] * (len(wholes) + 2),
        out_specs=[VMEM] * 2,
        compiler_params=PARAMS,
    )(*wholes, edge, taps)


def first_kernel(total, *refs):
    wholes, (edge, body, taps, out, blocks, acts) = refs[:-6], refs[-6:]
    width = wholes[0].shape[0] - 8
    ends = edge[:width]
    last = jnp.concatenate([ends[:, :WIDTH], body[...], ends[:, WIDTH:]], axis=1)
    values = [ref[:width] for ref in wholes] + [last]
    for k, block in enumerate(normed(values, first_gains(wholes, edge, width), total)):
        blocks[k] = block
    for k in range(len(values)):
        part = main_taps(blocks[k], taps, owner_of(k), acts.at[k % 2])
        out[...] = part if k == 0 else out[...] + part


def first_main(wholes, edge, body, taps):
    outs, total = taps.shape[1:]
    width, cells = wholes[0].shape[0] - 8, wholes[0].shape[1]
    return pl.pallas_call(
        lambda *refs: first_kernel(total, *refs),
        out_shape=jax.ShapeDtypeStruct((cells, outs), jnp.float32),
        in_specs=[VMEM] * (len(wholes) + 3),
        out_specs=VMEM,
        scratch_shapes=[
            pltpu.VMEM((len(wholes) + 1, cells, width), jnp.bfloat16),
            pltpu.VMEM((2, 3, cells + 2 * WIDTH, width), jnp.bfloat16),
        ],
        compiler_params=PARAMS,
    )(*wholes, edge, body, taps)


def part_kernel(k, block, taps, *refs):
    before, outs, acts = refs[:-4], refs[-4:-1], refs[-1]
    parts = [main_taps(block[...], taps, owner_of(k), acts), *edge_taps(block[...], taps, owner_of(k))]
    for place, part in enumerate(parts):
        outs[place][...] = before[place][...] + part if before else part


def second_part(k, block, taps, before):
    cells, width = block.shape
    outs = taps.shape[1]
    return pl.pallas_call(
        lambda *refs: part_kernel(k, *refs),
        out_shape=[jax.ShapeDtypeStruct((size, outs), jnp.float32) for size in (cells, WIDTH, WIDTH)],
        in_specs=[VMEM] * (2 + len(before)),
        out_specs=[VMEM] * 3,
        input_output_aliases={2 + i: i for i in range(len(before))},
        scratch_shapes=[pltpu.VMEM((3, cells + 2 * WIDTH, width), jnp.bfloat16)],
        compiler_params=PARAMS,
    )(block, taps, *before)


def second_edge_kernel(k, edge, taps, above, below, first, second):
    parts = edge_taps(edge[...], taps, owner_of(k))
    first[...], second[...] = to_swap(above[...] + parts[0], below[...] + parts[1])


def second_edge(k, edge, taps, above, below):
    return pl.pallas_call(
        lambda *refs: second_edge_kernel(k, *refs),
        out_shape=[jax.ShapeDtypeStruct(above.shape, above.dtype)] * 2,
        in_specs=[VMEM] * 4,
        out_specs=[VMEM] * 2,
        compiler_params=PARAMS,
    )(edge, taps, above, below)


def second_main_kernel(k, edge, body, taps, before, out, acts):
    block = jnp.concatenate([edge[:WIDTH], body[...], edge[WIDTH:]], axis=0)
    out[...] = before[...] + main_taps(block, taps, owner_of(k), acts)


def second_main(k, edge, body, taps, before):
    return pl.pallas_call(
        lambda *refs: second_main_kernel(k, *refs),
        out_shape=jax.ShapeDtypeStruct(before.shape, before.dtype),
        in_specs=[VMEM] * 4,
        out_specs=VMEM,
        input_output_aliases={3: 0},
        scratch_shapes=[pltpu.VMEM((3, before.shape[0] + 2 * WIDTH, edge.shape[1]), jnp.bfloat16)],
        compiler_params=PARAMS,
    )(edge, body, taps, before)


def to_swap(above, below):
    even = lax.axis_index("rows") % 2 == 0
    return jnp.where(even, below, above), jnp.where(even, above, below)


def joined(main, first, second, bias):
    row = lax.axis_index("rows")
    even, top, low = row % 2 == 0, row == 0, row == lax.axis_size("rows") - 1
    above = jnp.where(even, second[...], first[...])
    below = jnp.where(even, first[...], second[...])
    above, below = jnp.where(top, 0.0, above), jnp.where(low, 0.0, below)
    end = main.shape[0] - WIDTH
    rows = [main[:WIDTH] + above, main[WIDTH:end], main[end:] + below]
    return jnp.concatenate(rows, axis=0) + bias[...]


def middle_kernel(main, first, second, bias, out, squares):
    middle = joined(main, first, second, bias)
    out[...] = middle
    squares[...] = row_of(jnp.sum(middle * middle, axis=1, keepdims=True))


def out_kernel(main, first, second, bias, source, out):
    result = joined(main, first, second, bias).T + source[...].astype(jnp.float32)
    out[...] = result.astype(out.dtype)


def act_kernel(total, values, gain, *refs):
    sums, (out, edge, body) = refs[:-3], refs[-3:]
    inverse = column_of(1.0 / jnp.sqrt(sum(ref[...] for ref in sums) / total + 1e-6))
    result = silu(values[...] * gain[...] * inverse).astype(out.dtype)
    end = result.shape[0] - WIDTH
    out[...] = result
    edge[:WIDTH], edge[WIDTH:] = result[:WIDTH], result[end:]
    body[...] = result[WIDTH:end]


def act(values, gain, sums, total):
    return pl.pallas_call(
        lambda *refs: act_kernel(total, *refs),
        out_shape=[
            jax.ShapeDtypeStruct((size, values.shape[1]), jnp.bfloat16)
            for size in (values.shape[0], 2 * WIDTH, values.shape[0] - 2 * WIDTH)
        ],
        in_specs=[VMEM] * (2 + len(sums)),
        out_specs=[VMEM] * 3,
        compiler_params=PARAMS,
    )(values, gain, *sums)


def with_row_neighbours(sends):
    count = lax.axis_size("rows")
    rounds = []
    for begin, send in enumerate(sends):
        pairs = [(i, (i + 1) % count) for i in range(begin, count, 2)]
        rounds.append(lax.ppermute(send, "rows", pairs + [(b, a) for a, b in pairs]))
    return rounds


def swap(value, step):
    return lax.ppermute(value, "chan", [(i, i ^ step) for i in range(lax.axis_size("chan"))])


def gathered(block, edge, body):
    *steps, last = steps_of(lax.axis_size("chan"))
    blocks = [block] + [swap(block, step) for step in steps]
    return blocks, *[swap(v, last) for v in (edge, body)]


def resident(
    features, gain_first, weight_first, bias_first, gain_second, weight_second, bias_second
):
    channels, frames, cells = features.shape
    total = weight_first.shape[4]
    count = lax.axis_size("chan")
    source = features.reshape(channels, cells)
    taps = fetch(weight_first)
    blocks, edge, body = gathered(*to_send(source, gain_first.reshape(1, -1)))
    sends = first_edge(blocks, edge, taps)
    edges = with_row_neighbours(sends)
    main = first_main(blocks, edge, body, taps)
    middle, squares = pl.pallas_call(
        middle_kernel,
        out_shape=[
            jax.ShapeDtypeStruct((cells, channels), jnp.float32),
            jax.ShapeDtypeStruct((1, cells), jnp.float32),
        ],
        in_specs=[VMEM] * 4,
        out_specs=[VMEM] * 2,
        compiler_params=PARAMS,
    )(main, *edges, bias_first.reshape(1, -1))
    others = [swap(squares, step) for step in range(count - 1, 0, -1)]
    second = act(middle, gain_second.reshape(1, -1), [squares, *others], total)
    taps = fetch(weight_second)
    blocks, edge, body = gathered(*second)
    parts = ()
    for k, block in enumerate(blocks):
        parts = second_part(k, block, taps, parts)
    sends = second_edge(count - 1, edge, taps, *parts[1:])
    edges = with_row_neighbours(sends)
    main = second_main(count - 1, edge, body, taps, parts[0])
    out = pl.pallas_call(
        out_kernel,
        out_shape=jax.ShapeDtypeStruct((channels, cells), features.dtype),
        in_specs=[VMEM] * 5,
        out_specs=VMEM,
        compiler_params=PARAMS,
    )(main, *edges, bias_second.reshape(1, -1), source)
    return out.reshape(channels, frames, cells)


def padded(block, width):
    low = shift_along(block[..., block.shape[-1] - width :], "rows", 1)
    high = shift_along(block[..., :width], "rows", -1)
    return jnp.concatenate([low, block, high], axis=-1)


def activate(values, gain, total):
    mean_sq = lax.psum(jnp.sum(values * values, axis=0, keepdims=True), "chan") / total
    return jax.nn.silu(values * gain[:, None, None] / jnp.sqrt(mean_sq + 1e-06)).astype(jnp.bfloat16)


def convolve(block, kernel):
    whole = padded(lax.all_gather(block, "chan", axis=0, tiled=True), WIDTH)
    channels, frames, cells = whole.shape
    grid = whole.reshape(1, channels, frames, cells // WIDTH, WIDTH)
    result = lax.conv_general_dilated(
        grid,
        kernel,
        (1, 1, 1),
        ((2, 0), (0, 0), (1, 1)),
        dimension_numbers=("NCDHW", "DHWOI", "NCDHW"),
        preferred_element_type=jnp.float32,
    )
    return result[0].reshape(kernel.shape[3], frames, cells - 2 * WIDTH)


def general(features, gain_first, weight_first, bias_first, gain_second, weight_second, bias_second):
    total = weight_first.shape[4]
    source = features.astype(jnp.float32)
    middle = convolve(activate(source, gain_first, total), weight_first) + bias_first[:, None, None]
    result = convolve(activate(middle, gain_second, total), weight_second)
    return (source + result + bias_second[:, None, None]).astype(jnp.bfloat16)


def on_device(
    features, gain_first, weight_first, bias_first, gain_second, weight_second, bias_second
):
    channels, frames, cells = features.shape
    chan, rows = lax.axis_size("chan"), lax.axis_size("rows")
    narrow = channels % LANES or cells < 3 * WIDTH or channels > cells
    if frames != 1 or narrow or chan < 2 or chan & (chan - 1) or rows % 2:
        return general(
            features, gain_first, weight_first, bias_first, gain_second, weight_second, bias_second
        )
    out = resident(
        features, gain_first, weight_first, bias_first, gain_second, weight_second, bias_second
    )
    return out


def solution(mesh):
    in_specs = (
        P("chan", None, "rows"),
        P("chan"),
        P(None, None, None, "chan", None),
        P("chan"),
        P("chan"),
        P(None, None, None, "chan", None),
        P("chan"),
    )
    return jax.shard_map(
        on_device, mesh=mesh, in_specs=in_specs, out_specs=P("chan", None, "rows"), check_vma=False
    )
```

```python
import jax
import jax.numpy as jnp
from jax import lax
from jax.experimental import pallas as pl
from jax.experimental.pallas import tpu as pltpu
from jax.sharding import PartitionSpec as P

WIDTH = 64
LANES = 128


def shift_along(block, axis, step):
    count = lax.axis_size(axis)
    pairs = [(i, i + step) for i in range(count) if 0 <= i + step < count]
    return lax.ppermute(block, axis, pairs)


VMEM = pl.BlockSpec(memory_space=pltpu.VMEM)
HBM = pl.BlockSpec(memory_space=pltpu.HBM)
PARAMS = pltpu.CompilerParams(vmem_limit_bytes=20 << 20)


def column_of(row):
    return jnp.broadcast_to(row, (LANES, row.shape[1])).T[:, :1]


def row_of(column):
    return jnp.broadcast_to(column, (column.shape[0], LANES)).T[:1]


def silu(values):
    return values / (1.0 + jnp.exp(-values))


def filter_copies(frame, weights, taps, sems):
    return [
        pltpu.make_async_copy(weights.at[frame, q, s], taps.at[q * 3 + s], sems.at[q * 3 + s])
        for q in range(3)
        for s in range(3)
    ]


def fetch_kernel(frame, weights, taps, sems):
    copies = filter_copies(frame, weights, taps, sems)
    for copy in copies:
        copy.start()
    for copy in copies:
        copy.wait()


def fetch(weights):
    outs, total = weights.shape[3:]
    return pl.pallas_call(
        lambda *refs: fetch_kernel(weights.shape[0] - 1, *refs),
        out_shape=pltpu.VMEM((9, outs, total), weights.dtype),
        in_specs=[HBM],
        out_specs=VMEM,
        scratch_shapes=[pltpu.SemaphoreType.DMA((9,))],
        compiler_params=PARAMS,
    )(pltpu.with_memory_space_constraint(weights, pltpu.HBM))


def shifted(values):
    cells = values.shape[0]
    column = lax.broadcasted_iota(jnp.int32, (cells, 1), 0) % WIDTH
    before = jnp.where(column == 0, 0.0, pltpu.roll(values, 1, 0))
    after = jnp.where(column == WIDTH - 1, 0.0, pltpu.roll(values, cells - 1, 0))
    return [part.astype(jnp.bfloat16) for part in (before, values, after)]


def matmul(left, right):
    return lax.dot_general(
        jnp.concatenate(left, axis=1),
        jnp.concatenate(right, axis=1),
        (((1,), (1,)), ((), ())),
        preferred_element_type=jnp.float32,
    )


def steps_of(count):
    return sorted(range(1, count), key=lambda step: (step != count // 2, step))


def owner_of(k):
    return lax.axis_index("chan") ^ [0, *steps_of(lax.axis_size("chan"))][k]


def lanes_of(owner, width):
    return pl.ds(pl.multiple_of(owner * width, width), width)


def main_taps(block, taps, owner, acts):
    cells, width = block.shape
    zeros = jnp.zeros((WIDTH, width), acts.dtype)
    for s, part in enumerate(shifted(block.astype(jnp.float32))):
        acts[s, :WIDTH] = zeros
        acts[s, WIDTH : WIDTH + cells] = part
        acts[s, WIDTH + cells :] = zeros
    lanes = lanes_of(owner, width)
    left = [acts[s, q * WIDTH : q * WIDTH + cells] for q in range(3) for s in range(3)]
    return matmul(left, [taps[t, :, lanes] for t in range(9)])


def edge_taps(block, taps, owner):
    cells, width = block.shape
    lanes = lanes_of(owner, width)
    above = matmul(shifted(block[:WIDTH].astype(jnp.float32)), [taps[6 + s, :, lanes] for s in range(3)])
    low = shifted(block[cells - WIDTH :].astype(jnp.float32))
    return above, matmul(low, [taps[s, :, lanes] for s in range(3)])


def thirds(value):
    parts = []
    for _ in range(3):
        parts.append(value.astype(jnp.bfloat16).astype(jnp.float32))
        value = value - parts[-1]
    return parts


def note_rows(values, lanes, rows):
    pieces = []
    for value in values:
        step = min(value.shape[1], lanes)
        for part in thirds(value):
            for k in range(0, value.shape[1], step):
                piece = part[:, k : k + step]
                if lanes > step:
                    piece = jnp.concatenate([piece, jnp.zeros((1, lanes - step), jnp.float32)], axis=1)
                pieces.append(piece)
    return jnp.concatenate([*pieces, jnp.zeros((rows - len(pieces), lanes), jnp.float32)], axis=0)


def noted(note, width, skip=0):
    step = min(width, note.shape[1])
    count = width // step
    rows = [note[skip + k : skip + k + 1, :step].astype(jnp.float32) for k in range(3 * count)]
    parts = [jnp.concatenate(rows[k * count : (k + 1) * count], axis=1) for k in range(3)]
    return (parts[0] + parts[1]) + parts[2]


def send_kernel(source, note, whole, edge, body, gain, sems):
    width, cells = source.shape
    copies = [
        pltpu.make_async_copy(source, whole.at[:width], sems.at[0]),
        pltpu.make_async_copy(note, gain, sems.at[1]),
    ]
    for copy in copies:
        copy.start()
    copies[1].wait()
    whole[width:] = note_rows([gain[...]], cells, whole.shape[0] - width).astype(whole.dtype)
    copies[0].wait()
    values = whole[:width].astype(jnp.float32)
    notes = [gain[...], jnp.sum(values * values, axis=0, keepdims=True)]
    edge[width:] = note_rows(notes, edge.shape[1], edge.shape[0] - width).astype(edge.dtype)
    edge[:width] = edges_in(whole[:width])
    body[...] = whole[:width, WIDTH : cells - WIDTH]


def edges_in(block):
    cells = block.shape[1]
    return jnp.concatenate([block[:, :WIDTH], block[:, cells - WIDTH :]], axis=1)


def to_send(block, gain):
    width, cells = block.shape
    pieces = 3 * (pl.cdiv(width, 2 * WIDTH) + cells // (2 * WIDTH))
    shapes = [(width + 8, cells), (width + 8 * pl.cdiv(pieces, 8), 2 * WIDTH), (width, cells - 2 * WIDTH)]
    return pl.pallas_call(
        send_kernel,
        out_shape=[pltpu.VMEM(shape, block.dtype) for shape in shapes],
        in_specs=[HBM] * 2,
        out_specs=[VMEM] * 3,
        scratch_shapes=[pltpu.VMEM(gain.shape, gain.dtype), pltpu.SemaphoreType.DMA((2,))],
        compiler_params=PARAMS,
    )(*[pltpu.with_memory_space_constraint(value, pltpu.HBM) for value in (block, gain)])


def normed(values, gains, total):
    values = [value.astype(jnp.float32) for value in values]
    squares = sum(jnp.sum(value * value, axis=0, keepdims=True) for value in values)
    inverse = column_of(1.0 / jnp.sqrt(squares / total + 1e-6))
    return [silu(value.T * gain * inverse).astype(jnp.bfloat16) for value, gain in zip(values, gains)]


def first_gains(wholes, edge, width):
    return [noted(ref[width:], width) for ref in (*wholes, edge)]


def first_edge_kernel(total, *refs):
    wholes, (edge, taps, first, second) = refs[:-4], refs[-4:]
    width = wholes[0].shape[0] - 8
    values = [edges_in(ref[:width]) for ref in wholes] + [edge[:width]]
    blocks = normed(values, first_gains(wholes, edge, width), total)
    parts = [edge_taps(block, taps, owner_of(k)) for k, block in enumerate(blocks)]
    first[...], second[...] = to_swap(sum(p[0] for p in parts), sum(p[1] for p in parts))


def first_edge(wholes, edge, taps):
    outs, total = taps.shape[1:]
    return pl.pallas_call(
        lambda *refs: first_edge_kernel(total, *refs),
        out_shape=[jax.ShapeDtypeStruct((WIDTH, outs), jnp.float32)] * 2,
        in_specs=[VMEM] * (len(wholes) + 2),
        out_specs=[VMEM] * 2,
        compiler_params=PARAMS,
    )(*wholes, edge, taps)


def first_upper_kernel(total, *refs):
    wholes, (edge, taps, out, squares, acts) = refs[:-5], refs[-5:]
    width, cells = wholes[0].shape[0] - 8, wholes[0].shape[1]
    values = [ref[:width].astype(jnp.float32) for ref in wholes]
    sums = noted(edge[width:], cells, 3 * pl.cdiv(width, edge.shape[1]))
    sums = sum(jnp.sum(value * value, axis=0, keepdims=True) for value in values) + sums
    squares[...] = sums
    inverse = column_of(1.0 / jnp.sqrt(sums / total + 1e-6))
    for k, value in enumerate(values):
        block = silu(value.T * noted(wholes[k][width:], width) * inverse).astype(jnp.bfloat16)
        part = main_taps(block, taps, owner_of(k), acts.at[k % 2])
        out[...] = part if k == 0 else out[...] + part


def first_upper(wholes, edge, taps):
    outs, total = taps.shape[1:]
    width, cells = wholes[0].shape[0] - 8, wholes[0].shape[1]
    return pl.pallas_call(
        lambda *refs: first_upper_kernel(total, *refs),
        out_shape=[
            jax.ShapeDtypeStruct((cells, outs), jnp.float32),
            jax.ShapeDtypeStruct((1, cells), jnp.float32),
        ],
        in_specs=[VMEM] * (len(wholes) + 2),
        out_specs=[VMEM] * 2,
        scratch_shapes=[pltpu.VMEM((2, 3, cells + 2 * WIDTH, width), jnp.bfloat16)],
        compiler_params=PARAMS,
    )(*wholes, edge, taps)


def first_main_kernel(k, total, edge, body, taps, squares, before, out, acts):
    width = body.shape[0]
    ends = edge[:width]
    last = jnp.concatenate([ends[:, :WIDTH], body[...], ends[:, WIDTH:]], axis=1).astype(jnp.float32)
    inverse = column_of(1.0 / jnp.sqrt(squares[...] / total + 1e-6))
    block = silu(last.T * noted(edge[width:], width) * inverse).astype(jnp.bfloat16)
    out[...] = before[...] + main_taps(block, taps, owner_of(k), acts)


def first_main(k, edge, body, taps, squares, before):
    total = taps.shape[2]
    return pl.pallas_call(
        lambda *refs: first_main_kernel(k, total, *refs),
        out_shape=jax.ShapeDtypeStruct(before.shape, before.dtype),
        in_specs=[VMEM] * 5,
        out_specs=VMEM,
        input_output_aliases={4: 0},
        scratch_shapes=[pltpu.VMEM((3, before.shape[0] + 2 * WIDTH, body.shape[0]), jnp.bfloat16)],
        compiler_params=PARAMS,
    )(edge, body, taps, squares, before)


def part_kernel(k, block, taps, *refs):
    before, outs, acts = refs[:-4], refs[-4:-1], refs[-1]
    parts = [main_taps(block[...], taps, owner_of(k), acts), *edge_taps(block[...], taps, owner_of(k))]
    for place, part in enumerate(parts):
        outs[place][...] = before[place][...] + part if before else part


def second_part(k, block, taps, before):
    cells, width = block.shape
    outs = taps.shape[1]
    return pl.pallas_call(
        lambda *refs: part_kernel(k, *refs),
        out_shape=[jax.ShapeDtypeStruct((size, outs), jnp.float32) for size in (cells, WIDTH, WIDTH)],
        in_specs=[VMEM] * (2 + len(before)),
        out_specs=[VMEM] * 3,
        input_output_aliases={2 + i: i for i in range(len(before))},
        scratch_shapes=[pltpu.VMEM((3, cells + 2 * WIDTH, width), jnp.bfloat16)],
        compiler_params=PARAMS,
    )(block, taps, *before)


def second_edge_kernel(k, edge, taps, above, below, first, second):
    parts = edge_taps(edge[...], taps, owner_of(k))
    first[...], second[...] = to_swap(above[...] + parts[0], below[...] + parts[1])


def second_edge(k, edge, taps, above, below):
    return pl.pallas_call(
        lambda *refs: second_edge_kernel(k, *refs),
        out_shape=[jax.ShapeDtypeStruct(above.shape, above.dtype)] * 2,
        in_specs=[VMEM] * 4,
        out_specs=[VMEM] * 2,
        compiler_params=PARAMS,
    )(edge, taps, above, below)


def second_main_kernel(k, edge, body, taps, before, out, acts):
    block = jnp.concatenate([edge[:WIDTH], body[...], edge[WIDTH:]], axis=0)
    out[...] = before[...] + main_taps(block, taps, owner_of(k), acts)


def second_main(k, edge, body, taps, before):
    return pl.pallas_call(
        lambda *refs: second_main_kernel(k, *refs),
        out_shape=jax.ShapeDtypeStruct(before.shape, before.dtype),
        in_specs=[VMEM] * 4,
        out_specs=VMEM,
        input_output_aliases={3: 0},
        scratch_shapes=[pltpu.VMEM((3, before.shape[0] + 2 * WIDTH, edge.shape[1]), jnp.bfloat16)],
        compiler_params=PARAMS,
    )(edge, body, taps, before)


def to_swap(above, below):
    even = lax.axis_index("rows") % 2 == 0
    return jnp.where(even, below, above), jnp.where(even, above, below)


def joined(main, first, second, bias):
    row = lax.axis_index("rows")
    even, top, low = row % 2 == 0, row == 0, row == lax.axis_size("rows") - 1
    above = jnp.where(even, second[...], first[...])
    below = jnp.where(even, first[...], second[...])
    above, below = jnp.where(top, 0.0, above), jnp.where(low, 0.0, below)
    end = main.shape[0] - WIDTH
    rows = [main[:WIDTH] + above, main[WIDTH:end], main[end:] + below]
    return jnp.concatenate(rows, axis=0) + bias[...]


def middle_kernel(main, first, second, bias, out, squares):
    middle = joined(main, first, second, bias)
    out[...] = middle
    squares[...] = row_of(jnp.sum(middle * middle, axis=1, keepdims=True))


def out_kernel(main, first, second, bias, source, out):
    result = joined(main, first, second, bias).T + source[...].astype(jnp.float32)
    out[...] = result.astype(out.dtype)


def act_kernel(total, values, gain, *refs):
    sums, (out, edge, body) = refs[:-3], refs[-3:]
    inverse = column_of(1.0 / jnp.sqrt(sum(ref[...] for ref in sums) / total + 1e-6))
    result = silu(values[...] * gain[...] * inverse).astype(out.dtype)
    end = result.shape[0] - WIDTH
    out[...] = result
    edge[:WIDTH], edge[WIDTH:] = result[:WIDTH], result[end:]
    body[...] = result[WIDTH:end]


def act(values, gain, sums, total):
    return pl.pallas_call(
        lambda *refs: act_kernel(total, *refs),
        out_shape=[
            jax.ShapeDtypeStruct((size, values.shape[1]), jnp.bfloat16)
            for size in (values.shape[0], 2 * WIDTH, values.shape[0] - 2 * WIDTH)
        ],
        in_specs=[VMEM] * (2 + len(sums)),
        out_specs=[VMEM] * 3,
        compiler_params=PARAMS,
    )(values, gain, *sums)


def with_row_neighbours(sends):
    count = lax.axis_size("rows")
    rounds = []
    for begin, send in enumerate(sends):
        pairs = [(i, (i + 1) % count) for i in range(begin, count, 2)]
        rounds.append(lax.ppermute(send, "rows", pairs + [(b, a) for a, b in pairs]))
    return rounds


def swap(value, step):
    return lax.ppermute(value, "chan", [(i, i ^ step) for i in range(lax.axis_size("chan"))])


def gathered(block, edge, body):
    *steps, last = steps_of(lax.axis_size("chan"))
    blocks = [block] + [swap(block, step) for step in steps]
    return blocks, *[swap(v, last) for v in (edge, body)]


def resident(
    features, gain_first, weight_first, bias_first, gain_second, weight_second, bias_second
):
    channels, frames, cells = features.shape
    total = weight_first.shape[4]
    count = lax.axis_size("chan")
    source = features.reshape(channels, cells)
    taps = fetch(weight_first)
    blocks, edge, body = gathered(*to_send(source, gain_first.reshape(1, -1)))
    sends = first_edge(blocks, edge, taps)
    edges = with_row_neighbours(sends)
    main, squares = first_upper(blocks, edge, taps)
    main = first_main(count - 1, edge, body, taps, squares, main)
    middle, squares = pl.pallas_call(
        middle_kernel,
        out_shape=[
            jax.ShapeDtypeStruct((cells, channels), jnp.float32),
            jax.ShapeDtypeStruct((1, cells), jnp.float32),
        ],
        in_specs=[VMEM] * 4,
        out_specs=[VMEM] * 2,
        compiler_params=PARAMS,
    )(main, *edges, bias_first.reshape(1, -1))
    others = [swap(squares, step) for step in range(count - 1, 0, -1)]
    second = act(middle, gain_second.reshape(1, -1), [squares, *others], total)
    taps = fetch(weight_second)
    blocks, edge, body = gathered(*second)
    parts = ()
    for k, block in enumerate(blocks):
        parts = second_part(k, block, taps, parts)
    sends = second_edge(count - 1, edge, taps, *parts[1:])
    edges = with_row_neighbours(sends)
    main = second_main(count - 1, edge, body, taps, parts[0])
    out = pl.pallas_call(
        out_kernel,
        out_shape=jax.ShapeDtypeStruct((channels, cells), features.dtype),
        in_specs=[VMEM] * 5,
        out_specs=VMEM,
        compiler_params=PARAMS,
    )(main, *edges, bias_second.reshape(1, -1), source)
    return out.reshape(channels, frames, cells)


def padded(block, width):
    low = shift_along(block[..., block.shape[-1] - width :], "rows", 1)
    high = shift_along(block[..., :width], "rows", -1)
    return jnp.concatenate([low, block, high], axis=-1)


def activate(values, gain, total):
    mean_sq = lax.psum(jnp.sum(values * values, axis=0, keepdims=True), "chan") / total
    return jax.nn.silu(values * gain[:, None, None] / jnp.sqrt(mean_sq + 1e-06)).astype(jnp.bfloat16)


def convolve(block, kernel):
    whole = padded(lax.all_gather(block, "chan", axis=0, tiled=True), WIDTH)
    channels, frames, cells = whole.shape
    grid = whole.reshape(1, channels, frames, cells // WIDTH, WIDTH)
    result = lax.conv_general_dilated(
        grid,
        kernel,
        (1, 1, 1),
        ((2, 0), (0, 0), (1, 1)),
        dimension_numbers=("NCDHW", "DHWOI", "NCDHW"),
        preferred_element_type=jnp.float32,
    )
    return result[0].reshape(kernel.shape[3], frames, cells - 2 * WIDTH)


def general(features, gain_first, weight_first, bias_first, gain_second, weight_second, bias_second):
    total = weight_first.shape[4]
    source = features.astype(jnp.float32)
    middle = convolve(activate(source, gain_first, total), weight_first) + bias_first[:, None, None]
    result = convolve(activate(middle, gain_second, total), weight_second)
    return (source + result + bias_second[:, None, None]).astype(jnp.bfloat16)


def on_device(
    features, gain_first, weight_first, bias_first, gain_second, weight_second, bias_second
):
    channels, frames, cells = features.shape
    chan, rows = lax.axis_size("chan"), lax.axis_size("rows")
    narrow = channels % LANES or cells < 3 * WIDTH or channels > cells
    if frames != 1 or narrow or chan < 2 or chan & (chan - 1) or rows % 2:
        return general(
            features, gain_first, weight_first, bias_first, gain_second, weight_second, bias_second
        )
    out = resident(
        features, gain_first, weight_first, bias_first, gain_second, weight_second, bias_second
    )
    return out


def solution(mesh):
    in_specs = (
        P("chan", None, "rows"),
        P("chan"),
        P(None, None, None, "chan", None),
        P("chan"),
        P("chan"),
        P(None, None, None, "chan", None),
        P("chan"),
    )
    return jax.shard_map(
        on_device, mesh=mesh, in_specs=in_specs, out_specs=P("chan", None, "rows"), check_vma=False
    )
```

```python
import jax
import jax.numpy as jnp
from jax import lax
from jax.experimental import pallas as pl
from jax.experimental.pallas import tpu as pltpu
from jax.sharding import PartitionSpec as P

WIDTH = 64
LANES = 128


def shift_along(block, axis, step):
    count = lax.axis_size(axis)
    pairs = [(i, i + step) for i in range(count) if 0 <= i + step < count]
    return lax.ppermute(block, axis, pairs)


VMEM = pl.BlockSpec(memory_space=pltpu.VMEM)
HBM = pl.BlockSpec(memory_space=pltpu.HBM)
PARAMS = pltpu.CompilerParams(vmem_limit_bytes=20 << 20)


def column_of(row):
    return jnp.broadcast_to(row, (LANES, row.shape[1])).T[:, :1]


def row_of(column):
    return jnp.broadcast_to(column, (column.shape[0], LANES)).T[:1]


def silu(values):
    return values / (1.0 + jnp.exp(-values))


def filter_copies(frame, weights, taps, sems):
    return [
        pltpu.make_async_copy(weights.at[frame, q, s], taps.at[q * 3 + s], sems.at[q * 3 + s])
        for q in range(3)
        for s in range(3)
    ]


def fetch_kernel(frame, weights, taps, sems):
    copies = filter_copies(frame, weights, taps, sems)
    for copy in copies:
        copy.start()
    for copy in copies:
        copy.wait()


def fetch(weights):
    outs, total = weights.shape[3:]
    return pl.pallas_call(
        lambda *refs: fetch_kernel(weights.shape[0] - 1, *refs),
        out_shape=pltpu.VMEM((9, outs, total), weights.dtype),
        in_specs=[HBM],
        out_specs=VMEM,
        scratch_shapes=[pltpu.SemaphoreType.DMA((9,))],
        compiler_params=PARAMS,
    )(pltpu.with_memory_space_constraint(weights, pltpu.HBM))


def shifted(values):
    cells = values.shape[0]
    column = lax.broadcasted_iota(jnp.int32, (cells, 1), 0) % WIDTH
    before = jnp.where(column == 0, 0.0, pltpu.roll(values, 1, 0))
    after = jnp.where(column == WIDTH - 1, 0.0, pltpu.roll(values, cells - 1, 0))
    return [part.astype(jnp.bfloat16) for part in (before, values, after)]


def matmul(left, right):
    return lax.dot_general(
        jnp.concatenate(left, axis=1),
        jnp.concatenate(right, axis=1),
        (((1,), (1,)), ((), ())),
        preferred_element_type=jnp.float32,
    )


def steps_of(count):
    return sorted(range(1, count), key=lambda step: (step != count // 2, step))


def owner_of(k):
    return lax.axis_index("chan") ^ [0, *steps_of(lax.axis_size("chan"))][k]


def lanes_of(owner, width):
    return pl.ds(pl.multiple_of(owner * width, width), width)


def main_taps(block, taps, owner, acts):
    cells, width = block.shape
    zeros = jnp.zeros((WIDTH, width), acts.dtype)
    for s, part in enumerate(shifted(block.astype(jnp.float32))):
        acts[s, :WIDTH] = zeros
        acts[s, WIDTH : WIDTH + cells] = part
        acts[s, WIDTH + cells :] = zeros
    lanes = lanes_of(owner, width)
    left = [acts[s, q * WIDTH : q * WIDTH + cells] for q in range(3) for s in range(3)]
    return matmul(left, [taps[t, :, lanes] for t in range(9)])


def edge_taps(block, taps, owner):
    cells, width = block.shape
    lanes = lanes_of(owner, width)
    above = matmul(shifted(block[:WIDTH].astype(jnp.float32)), [taps[6 + s, :, lanes] for s in range(3)])
    low = shifted(block[cells - WIDTH :].astype(jnp.float32))
    return above, matmul(low, [taps[s, :, lanes] for s in range(3)])


def thirds(value):
    parts = []
    for _ in range(3):
        parts.append(value.astype(jnp.bfloat16).astype(jnp.float32))
        value = value - parts[-1]
    return parts


def note_rows(values, lanes, rows):
    pieces = []
    for value in values:
        step = min(value.shape[1], lanes)
        for part in thirds(value):
            for k in range(0, value.shape[1], step):
                piece = part[:, k : k + step]
                if lanes > step:
                    piece = jnp.concatenate([piece, jnp.zeros((1, lanes - step), jnp.float32)], axis=1)
                pieces.append(piece)
    return jnp.concatenate([*pieces, jnp.zeros((rows - len(pieces), lanes), jnp.float32)], axis=0)


def noted(note, width, skip=0):
    step = min(width, note.shape[1])
    count = width // step
    rows = [note[skip + k : skip + k + 1, :step].astype(jnp.float32) for k in range(3 * count)]
    parts = [jnp.concatenate(rows[k * count : (k + 1) * count], axis=1) for k in range(3)]
    return (parts[0] + parts[1]) + parts[2]


def send_kernel(source, note, whole, gain, sems):
    width, cells = source.shape
    copies = [
        pltpu.make_async_copy(source, whole.at[:width], sems.at[0]),
        pltpu.make_async_copy(note, gain, sems.at[1]),
    ]
    for copy in copies:
        copy.start()
    copies[1].wait()
    whole[width:] = note_rows([gain[...]], cells, whole.shape[0] - width).astype(whole.dtype)
    copies[0].wait()


def rest_kernel(whole, edge, body):
    width, cells = body.shape[0], whole.shape[1]
    values = whole[:width].astype(jnp.float32)
    notes = [noted(whole[width:], width), jnp.sum(values * values, axis=0, keepdims=True)]
    edge[width:] = note_rows(notes, edge.shape[1], edge.shape[0] - width).astype(edge.dtype)
    edge[:width] = edges_in(whole[:width])
    body[...] = whole[:width, WIDTH : cells - WIDTH]


def edges_in(block):
    cells = block.shape[1]
    return jnp.concatenate([block[:, :WIDTH], block[:, cells - WIDTH :]], axis=1)


def to_send(block, gain):
    width, cells = block.shape
    return pl.pallas_call(
        send_kernel,
        out_shape=pltpu.VMEM((width + 8, cells), block.dtype),
        in_specs=[HBM] * 2,
        out_specs=VMEM,
        scratch_shapes=[pltpu.VMEM(gain.shape, gain.dtype), pltpu.SemaphoreType.DMA((2,))],
        compiler_params=PARAMS,
    )(*[pltpu.with_memory_space_constraint(value, pltpu.HBM) for value in (block, gain)])


def rest_of(whole):
    width, cells = whole.shape[0] - 8, whole.shape[1]
    pieces = 3 * (pl.cdiv(width, 2 * WIDTH) + cells // (2 * WIDTH))
    shapes = [(width + 8 * pl.cdiv(pieces, 8), 2 * WIDTH), (width, cells - 2 * WIDTH)]
    return pl.pallas_call(
        rest_kernel,
        out_shape=[pltpu.VMEM(shape, whole.dtype) for shape in shapes],
        in_specs=[VMEM],
        out_specs=[VMEM] * 2,
        compiler_params=PARAMS,
    )(whole)


def normed(values, gains, total):
    values = [value.astype(jnp.float32) for value in values]
    squares = sum(jnp.sum(value * value, axis=0, keepdims=True) for value in values)
    inverse = column_of(1.0 / jnp.sqrt(squares / total + 1e-6))
    return [silu(value.T * gain * inverse).astype(jnp.bfloat16) for value, gain in zip(values, gains)]


def first_gains(wholes, edge, width):
    return [noted(ref[width:], width) for ref in (*wholes, edge)]


def first_edge_kernel(total, *refs):
    wholes, (edge, taps, first, second) = refs[:-4], refs[-4:]
    width = wholes[0].shape[0] - 8
    values = [edges_in(ref[:width]) for ref in wholes] + [edge[:width]]
    blocks = normed(values, first_gains(wholes, edge, width), total)
    parts = [edge_taps(block, taps, owner_of(k)) for k, block in enumerate(blocks)]
    first[...], second[...] = to_swap(sum(p[0] for p in parts), sum(p[1] for p in parts))


def first_edge(wholes, edge, taps):
    outs, total = taps.shape[1:]
    return pl.pallas_call(
        lambda *refs: first_edge_kernel(total, *refs),
        out_shape=[jax.ShapeDtypeStruct((WIDTH, outs), jnp.float32)] * 2,
        in_specs=[VMEM] * (len(wholes) + 2),
        out_specs=[VMEM] * 2,
        compiler_params=PARAMS,
    )(*wholes, edge, taps)


def first_upper_kernel(total, *refs):
    wholes, (edge, taps, out, squares, acts) = refs[:-5], refs[-5:]
    width, cells = wholes[0].shape[0] - 8, wholes[0].shape[1]
    values = [ref[:width].astype(jnp.float32) for ref in wholes]
    sums = noted(edge[width:], cells, 3 * pl.cdiv(width, edge.shape[1]))
    sums = sum(jnp.sum(value * value, axis=0, keepdims=True) for value in values) + sums
    squares[...] = sums
    inverse = column_of(1.0 / jnp.sqrt(sums / total + 1e-6))
    for k, value in enumerate(values):
        block = silu(value.T * noted(wholes[k][width:], width) * inverse).astype(jnp.bfloat16)
        part = main_taps(block, taps, owner_of(k), acts.at[k % 2])
        out[...] = part if k == 0 else out[...] + part


def first_upper(wholes, edge, taps):
    outs, total = taps.shape[1:]
    width, cells = wholes[0].shape[0] - 8, wholes[0].shape[1]
    return pl.pallas_call(
        lambda *refs: first_upper_kernel(total, *refs),
        out_shape=[
            jax.ShapeDtypeStruct((cells, outs), jnp.float32),
            jax.ShapeDtypeStruct((1, cells), jnp.float32),
        ],
        in_specs=[VMEM] * (len(wholes) + 2),
        out_specs=[VMEM] * 2,
        scratch_shapes=[pltpu.VMEM((2, 3, cells + 2 * WIDTH, width), jnp.bfloat16)],
        compiler_params=PARAMS,
    )(*wholes, edge, taps)


def first_main_kernel(k, total, edge, body, taps, squares, before, out, acts):
    width = body.shape[0]
    ends = edge[:width]
    last = jnp.concatenate([ends[:, :WIDTH], body[...], ends[:, WIDTH:]], axis=1).astype(jnp.float32)
    inverse = column_of(1.0 / jnp.sqrt(squares[...] / total + 1e-6))
    block = silu(last.T * noted(edge[width:], width) * inverse).astype(jnp.bfloat16)
    out[...] = before[...] + main_taps(block, taps, owner_of(k), acts)


def first_main(k, edge, body, taps, squares, before):
    total = taps.shape[2]
    return pl.pallas_call(
        lambda *refs: first_main_kernel(k, total, *refs),
        out_shape=jax.ShapeDtypeStruct(before.shape, before.dtype),
        in_specs=[VMEM] * 5,
        out_specs=VMEM,
        input_output_aliases={4: 0},
        scratch_shapes=[pltpu.VMEM((3, before.shape[0] + 2 * WIDTH, body.shape[0]), jnp.bfloat16)],
        compiler_params=PARAMS,
    )(edge, body, taps, squares, before)


def part_kernel(k, block, taps, *refs):
    before, outs, acts = refs[:-4], refs[-4:-1], refs[-1]
    parts = [main_taps(block[...], taps, owner_of(k), acts), *edge_taps(block[...], taps, owner_of(k))]
    for place, part in enumerate(parts):
        outs[place][...] = before[place][...] + part if before else part


def second_part(k, block, taps, before):
    cells, width = block.shape
    outs = taps.shape[1]
    return pl.pallas_call(
        lambda *refs: part_kernel(k, *refs),
        out_shape=[jax.ShapeDtypeStruct((size, outs), jnp.float32) for size in (cells, WIDTH, WIDTH)],
        in_specs=[VMEM] * (2 + len(before)),
        out_specs=[VMEM] * 3,
        input_output_aliases={2 + i: i for i in range(len(before))},
        scratch_shapes=[pltpu.VMEM((3, cells + 2 * WIDTH, width), jnp.bfloat16)],
        compiler_params=PARAMS,
    )(block, taps, *before)


def second_edge_kernel(k, edge, taps, above, below, first, second):
    parts = edge_taps(edge[...], taps, owner_of(k))
    first[...], second[...] = to_swap(above[...] + parts[0], below[...] + parts[1])


def second_edge(k, edge, taps, above, below):
    return pl.pallas_call(
        lambda *refs: second_edge_kernel(k, *refs),
        out_shape=[jax.ShapeDtypeStruct(above.shape, above.dtype)] * 2,
        in_specs=[VMEM] * 4,
        out_specs=[VMEM] * 2,
        compiler_params=PARAMS,
    )(edge, taps, above, below)


def second_main_kernel(k, edge, body, taps, before, out, acts):
    block = jnp.concatenate([edge[:WIDTH], body[...], edge[WIDTH:]], axis=0)
    out[...] = before[...] + main_taps(block, taps, owner_of(k), acts)


def second_main(k, edge, body, taps, before):
    return pl.pallas_call(
        lambda *refs: second_main_kernel(k, *refs),
        out_shape=jax.ShapeDtypeStruct(before.shape, before.dtype),
        in_specs=[VMEM] * 4,
        out_specs=VMEM,
        input_output_aliases={3: 0},
        scratch_shapes=[pltpu.VMEM((3, before.shape[0] + 2 * WIDTH, edge.shape[1]), jnp.bfloat16)],
        compiler_params=PARAMS,
    )(edge, body, taps, before)


def to_swap(above, below):
    even = lax.axis_index("rows") % 2 == 0
    return jnp.where(even, below, above), jnp.where(even, above, below)


def joined(main, first, second, bias):
    row = lax.axis_index("rows")
    even, top, low = row % 2 == 0, row == 0, row == lax.axis_size("rows") - 1
    above = jnp.where(even, second[...], first[...])
    below = jnp.where(even, first[...], second[...])
    above, below = jnp.where(top, 0.0, above), jnp.where(low, 0.0, below)
    end = main.shape[0] - WIDTH
    rows = [main[:WIDTH] + above, main[WIDTH:end], main[end:] + below]
    return jnp.concatenate(rows, axis=0) + bias[...]


def middle_kernel(main, first, second, bias, out, squares):
    middle = joined(main, first, second, bias)
    out[...] = middle
    squares[...] = row_of(jnp.sum(middle * middle, axis=1, keepdims=True))


def out_kernel(main, first, second, bias, source, out):
    result = joined(main, first, second, bias).T + source[...].astype(jnp.float32)
    out[...] = result.astype(out.dtype)


def act_kernel(total, values, gain, *refs):
    sums, (out, edge, body) = refs[:-3], refs[-3:]
    inverse = column_of(1.0 / jnp.sqrt(sum(ref[...] for ref in sums) / total + 1e-6))
    result = silu(values[...] * gain[...] * inverse).astype(out.dtype)
    end = result.shape[0] - WIDTH
    out[...] = result
    edge[:WIDTH], edge[WIDTH:] = result[:WIDTH], result[end:]
    body[...] = result[WIDTH:end]


def act(values, gain, sums, total):
    return pl.pallas_call(
        lambda *refs: act_kernel(total, *refs),
        out_shape=[
            jax.ShapeDtypeStruct((size, values.shape[1]), jnp.bfloat16)
            for size in (values.shape[0], 2 * WIDTH, values.shape[0] - 2 * WIDTH)
        ],
        in_specs=[VMEM] * (2 + len(sums)),
        out_specs=[VMEM] * 3,
        compiler_params=PARAMS,
    )(values, gain, *sums)


def with_row_neighbours(sends):
    count = lax.axis_size("rows")
    rounds = []
    for begin, send in enumerate(sends):
        pairs = [(i, (i + 1) % count) for i in range(begin, count, 2)]
        rounds.append(lax.ppermute(send, "rows", pairs + [(b, a) for a, b in pairs]))
    return rounds


def swap(value, step):
    return lax.ppermute(value, "chan", [(i, i ^ step) for i in range(lax.axis_size("chan"))])


def gathered(block, edge, body):
    *steps, last = steps_of(lax.axis_size("chan"))
    blocks = [block] + [swap(block, step) for step in steps]
    return blocks, *[swap(v, last) for v in (edge, body)]


def resident(
    features, gain_first, weight_first, bias_first, gain_second, weight_second, bias_second
):
    channels, frames, cells = features.shape
    total = weight_first.shape[4]
    count = lax.axis_size("chan")
    source = features.reshape(channels, cells)
    taps = fetch(weight_first)
    whole = to_send(source, gain_first.reshape(1, -1))
    blocks, edge, body = gathered(whole, *rest_of(whole))
    sends = first_edge(blocks, edge, taps)
    edges = with_row_neighbours(sends)
    main, squares = first_upper(blocks, edge, taps)
    main = first_main(count - 1, edge, body, taps, squares, main)
    middle, squares = pl.pallas_call(
        middle_kernel,
        out_shape=[
            jax.ShapeDtypeStruct((cells, channels), jnp.float32),
            jax.ShapeDtypeStruct((1, cells), jnp.float32),
        ],
        in_specs=[VMEM] * 4,
        out_specs=[VMEM] * 2,
        compiler_params=PARAMS,
    )(main, *edges, bias_first.reshape(1, -1))
    others = [swap(squares, step) for step in range(count - 1, 0, -1)]
    second = act(middle, gain_second.reshape(1, -1), [squares, *others], total)
    taps = fetch(weight_second)
    blocks, edge, body = gathered(*second)
    parts = ()
    for k, block in enumerate(blocks):
        parts = second_part(k, block, taps, parts)
    sends = second_edge(count - 1, edge, taps, *parts[1:])
    edges = with_row_neighbours(sends)
    main = second_main(count - 1, edge, body, taps, parts[0])
    out = pl.pallas_call(
        out_kernel,
        out_shape=jax.ShapeDtypeStruct((channels, cells), features.dtype),
        in_specs=[VMEM] * 5,
        out_specs=VMEM,
        compiler_params=PARAMS,
    )(main, *edges, bias_second.reshape(1, -1), source)
    return out.reshape(channels, frames, cells)


def padded(block, width):
    low = shift_along(block[..., block.shape[-1] - width :], "rows", 1)
    high = shift_along(block[..., :width], "rows", -1)
    return jnp.concatenate([low, block, high], axis=-1)


def activate(values, gain, total):
    mean_sq = lax.psum(jnp.sum(values * values, axis=0, keepdims=True), "chan") / total
    return jax.nn.silu(values * gain[:, None, None] / jnp.sqrt(mean_sq + 1e-06)).astype(jnp.bfloat16)


def convolve(block, kernel):
    whole = padded(lax.all_gather(block, "chan", axis=0, tiled=True), WIDTH)
    channels, frames, cells = whole.shape
    grid = whole.reshape(1, channels, frames, cells // WIDTH, WIDTH)
    result = lax.conv_general_dilated(
        grid,
        kernel,
        (1, 1, 1),
        ((2, 0), (0, 0), (1, 1)),
        dimension_numbers=("NCDHW", "DHWOI", "NCDHW"),
        preferred_element_type=jnp.float32,
    )
    return result[0].reshape(kernel.shape[3], frames, cells - 2 * WIDTH)


def general(features, gain_first, weight_first, bias_first, gain_second, weight_second, bias_second):
    total = weight_first.shape[4]
    source = features.astype(jnp.float32)
    middle = convolve(activate(source, gain_first, total), weight_first) + bias_first[:, None, None]
    result = convolve(activate(middle, gain_second, total), weight_second)
    return (source + result + bias_second[:, None, None]).astype(jnp.bfloat16)


def on_device(
    features, gain_first, weight_first, bias_first, gain_second, weight_second, bias_second
):
    channels, frames, cells = features.shape
    chan, rows = lax.axis_size("chan"), lax.axis_size("rows")
    narrow = channels % LANES or cells < 3 * WIDTH or channels > cells
    if frames != 1 or narrow or chan < 2 or chan & (chan - 1) or rows % 2:
        return general(
            features, gain_first, weight_first, bias_first, gain_second, weight_second, bias_second
        )
    out = resident(
        features, gain_first, weight_first, bias_first, gain_second, weight_second, bias_second
    )
    return out


def solution(mesh):
    in_specs = (
        P("chan", None, "rows"),
        P("chan"),
        P(None, None, None, "chan", None),
        P("chan"),
        P("chan"),
        P(None, None, None, "chan", None),
        P("chan"),
    )
    return jax.shard_map(
        on_device, mesh=mesh, in_specs=in_specs, out_specs=P("chan", None, "rows"), check_vma=False
    )
```

```python
import jax
import jax.numpy as jnp
from jax import lax
from jax.experimental import pallas as pl
from jax.experimental.pallas import tpu as pltpu
from jax.sharding import PartitionSpec as P

WIDTH = 64
LANES = 128


def shift_along(block, axis, step):
    count = lax.axis_size(axis)
    pairs = [(i, i + step) for i in range(count) if 0 <= i + step < count]
    return lax.ppermute(block, axis, pairs)


VMEM = pl.BlockSpec(memory_space=pltpu.VMEM)
HBM = pl.BlockSpec(memory_space=pltpu.HBM)
PARAMS = pltpu.CompilerParams(vmem_limit_bytes=20 << 20)


def column_of(row):
    return jnp.broadcast_to(row, (LANES, row.shape[1])).T[:, :1]


def row_of(column):
    return jnp.broadcast_to(column, (column.shape[0], LANES)).T[:1]


def silu(values):
    return values / (1.0 + jnp.exp(-values))


def filter_copies(frame, weights, taps, sems):
    return [
        pltpu.make_async_copy(weights.at[frame, q, s], taps.at[q * 3 + s], sems.at[q * 3 + s])
        for q in range(3)
        for s in range(3)
    ]


def fetch_kernel(frame, weights, taps, sems):
    copies = filter_copies(frame, weights, taps, sems)
    for copy in copies:
        copy.start()
    for copy in copies:
        copy.wait()


def fetch(weights):
    outs, total = weights.shape[3:]
    return pl.pallas_call(
        lambda *refs: fetch_kernel(weights.shape[0] - 1, *refs),
        out_shape=pltpu.VMEM((9, outs, total), weights.dtype),
        in_specs=[HBM],
        out_specs=VMEM,
        scratch_shapes=[pltpu.SemaphoreType.DMA((9,))],
        compiler_params=PARAMS,
    )(pltpu.with_memory_space_constraint(weights, pltpu.HBM))


def shifted(values):
    cells = values.shape[0]
    column = lax.broadcasted_iota(jnp.int32, (cells, 1), 0) % WIDTH
    before = jnp.where(column == 0, 0.0, pltpu.roll(values, 1, 0))
    after = jnp.where(column == WIDTH - 1, 0.0, pltpu.roll(values, cells - 1, 0))
    return [part.astype(jnp.bfloat16) for part in (before, values, after)]


def matmul(left, right):
    return lax.dot_general(
        jnp.concatenate(left, axis=1),
        jnp.concatenate(right, axis=1),
        (((1,), (1,)), ((), ())),
        preferred_element_type=jnp.float32,
    )


def steps_of(count):
    return sorted(range(1, count), key=lambda step: (step != count // 2, step))


def owner_of(k):
    return lax.axis_index("chan") ^ [0, *steps_of(lax.axis_size("chan"))][k]


def lanes_of(owner, width):
    return pl.ds(pl.multiple_of(owner * width, width), width)


def main_taps(block, taps, owner, acts):
    cells, width = block.shape
    zeros = jnp.zeros((WIDTH, width), acts.dtype)
    for s, part in enumerate(shifted(block.astype(jnp.float32))):
        acts[s, :WIDTH] = zeros
        acts[s, WIDTH : WIDTH + cells] = part
        acts[s, WIDTH + cells :] = zeros
    lanes = lanes_of(owner, width)
    left = [acts[s, q * WIDTH : q * WIDTH + cells] for q in range(3) for s in range(3)]
    return matmul(left, [taps[t, :, lanes] for t in range(9)])


def edge_taps(block, taps, owner):
    cells, width = block.shape
    lanes = lanes_of(owner, width)
    above = matmul(shifted(block[:WIDTH].astype(jnp.float32)), [taps[6 + s, :, lanes] for s in range(3)])
    low = shifted(block[cells - WIDTH :].astype(jnp.float32))
    return above, matmul(low, [taps[s, :, lanes] for s in range(3)])


def thirds(value):
    parts = []
    for _ in range(3):
        parts.append(value.astype(jnp.bfloat16).astype(jnp.float32))
        value = value - parts[-1]
    return parts


def note_rows(values, lanes, rows):
    pieces = []
    for value in values:
        step = min(value.shape[1], lanes)
        for part in thirds(value):
            for k in range(0, value.shape[1], step):
                piece = part[:, k : k + step]
                if lanes > step:
                    piece = jnp.concatenate([piece, jnp.zeros((1, lanes - step), jnp.float32)], axis=1)
                pieces.append(piece)
    return jnp.concatenate([*pieces, jnp.zeros((rows - len(pieces), lanes), jnp.float32)], axis=0)


def noted(note, width, skip=0):
    step = min(width, note.shape[1])
    count = width // step
    rows = [note[skip + k : skip + k + 1, :step].astype(jnp.float32) for k in range(3 * count)]
    parts = [jnp.concatenate(rows[k * count : (k + 1) * count], axis=1) for k in range(3)]
    return (parts[0] + parts[1]) + parts[2]


def send_kernel(source, note, whole, gain, sems):
    width, cells = source.shape
    copies = [
        pltpu.make_async_copy(source, whole.at[:width], sems.at[0]),
        pltpu.make_async_copy(note, gain, sems.at[1]),
    ]
    for copy in copies:
        copy.start()
    copies[1].wait()
    whole[width:] = note_rows([gain[...]], cells, whole.shape[0] - width).astype(whole.dtype)
    copies[0].wait()


def rest_kernel(whole, edge, body):
    width, cells = body.shape[0], whole.shape[1]
    values = whole[:width].astype(jnp.float32)
    notes = [noted(whole[width:], width), jnp.sum(values * values, axis=0, keepdims=True)]
    edge[width:] = note_rows(notes, edge.shape[1], edge.shape[0] - width).astype(edge.dtype)
    edge[:width] = edges_in(whole[:width])
    body[...] = whole[:width, WIDTH : cells - WIDTH]


def edges_in(block):
    cells = block.shape[1]
    return jnp.concatenate([block[:, :WIDTH], block[:, cells - WIDTH :]], axis=1)


def to_send(block, gain):
    width, cells = block.shape
    return pl.pallas_call(
        send_kernel,
        out_shape=pltpu.VMEM((width + 8, cells), block.dtype),
        in_specs=[HBM] * 2,
        out_specs=VMEM,
        scratch_shapes=[pltpu.VMEM(gain.shape, gain.dtype), pltpu.SemaphoreType.DMA((2,))],
        compiler_params=PARAMS,
    )(*[pltpu.with_memory_space_constraint(value, pltpu.HBM) for value in (block, gain)])


def rest_of(whole):
    width, cells = whole.shape[0] - 8, whole.shape[1]
    pieces = 3 * (pl.cdiv(width, 2 * WIDTH) + cells // (2 * WIDTH))
    shapes = [(width + 8 * pl.cdiv(pieces, 8), 2 * WIDTH), (width, cells - 2 * WIDTH)]
    return pl.pallas_call(
        rest_kernel,
        out_shape=[pltpu.VMEM(shape, whole.dtype) for shape in shapes],
        in_specs=[VMEM],
        out_specs=[VMEM] * 2,
        compiler_params=PARAMS,
    )(whole)


def normed(values, gains, total):
    values = [value.astype(jnp.float32) for value in values]
    squares = sum(jnp.sum(value * value, axis=0, keepdims=True) for value in values)
    inverse = column_of(1.0 / jnp.sqrt(squares / total + 1e-6))
    return [silu(value.T * gain * inverse).astype(jnp.bfloat16) for value, gain in zip(values, gains)]


def first_gains(wholes, edge, width):
    return [noted(ref[width:], width) for ref in (*wholes, edge)]


def first_edge_kernel(total, *refs):
    wholes, (edge, taps, first, second) = refs[:-4], refs[-4:]
    width = wholes[0].shape[0] - 8
    values = [edges_in(ref[:width]) for ref in wholes] + [edge[:width]]
    blocks = normed(values, first_gains(wholes, edge, width), total)
    parts = [edge_taps(block, taps, owner_of(k)) for k, block in enumerate(blocks)]
    first[...], second[...] = to_swap(sum(p[0] for p in parts), sum(p[1] for p in parts))


def first_edge(wholes, edge, taps):
    outs, total = taps.shape[1:]
    return pl.pallas_call(
        lambda *refs: first_edge_kernel(total, *refs),
        out_shape=[jax.ShapeDtypeStruct((WIDTH, outs), jnp.float32)] * 2,
        in_specs=[VMEM] * (len(wholes) + 2),
        out_specs=[VMEM] * 2,
        compiler_params=PARAMS,
    )(*wholes, edge, taps)


def first_upper_kernel(total, *refs):
    wholes, (edge, taps, out, squares, acts) = refs[:-5], refs[-5:]
    width, cells = wholes[0].shape[0] - 8, wholes[0].shape[1]
    values = [ref[:width].astype(jnp.float32) for ref in wholes]
    sums = noted(edge[width:], cells, 3 * pl.cdiv(width, edge.shape[1]))
    sums = sum(jnp.sum(value * value, axis=0, keepdims=True) for value in values) + sums
    squares[...] = sums
    inverse = column_of(1.0 / jnp.sqrt(sums / total + 1e-6))
    for k, value in enumerate(values):
        block = silu(value.T * noted(wholes[k][width:], width) * inverse).astype(jnp.bfloat16)
        part = main_taps(block, taps, owner_of(k), acts.at[k % 2])
        out[...] = part if k == 0 else out[...] + part


def first_upper(wholes, edge, taps):
    outs, total = taps.shape[1:]
    width, cells = wholes[0].shape[0] - 8, wholes[0].shape[1]
    return pl.pallas_call(
        lambda *refs: first_upper_kernel(total, *refs),
        out_shape=[
            jax.ShapeDtypeStruct((cells, outs), jnp.float32),
            jax.ShapeDtypeStruct((1, cells), jnp.float32),
        ],
        in_specs=[VMEM] * (len(wholes) + 2),
        out_specs=[VMEM] * 2,
        scratch_shapes=[pltpu.VMEM((2, 3, cells + 2 * WIDTH, width), jnp.bfloat16)],
        compiler_params=PARAMS,
    )(*wholes, edge, taps)


def first_main_kernel(k, total, edge, body, taps, squares, before, out, acts):
    width = body.shape[0]
    ends = edge[:width]
    last = jnp.concatenate([ends[:, :WIDTH], body[...], ends[:, WIDTH:]], axis=1).astype(jnp.float32)
    inverse = column_of(1.0 / jnp.sqrt(squares[...] / total + 1e-6))
    block = silu(last.T * noted(edge[width:], width) * inverse).astype(jnp.bfloat16)
    out[...] = before[...] + main_taps(block, taps, owner_of(k), acts)


def first_main(k, edge, body, taps, squares, before):
    total = taps.shape[2]
    return pl.pallas_call(
        lambda *refs: first_main_kernel(k, total, *refs),
        out_shape=jax.ShapeDtypeStruct(before.shape, before.dtype),
        in_specs=[VMEM] * 5,
        out_specs=VMEM,
        input_output_aliases={4: 0},
        scratch_shapes=[pltpu.VMEM((3, before.shape[0] + 2 * WIDTH, body.shape[0]), jnp.bfloat16)],
        compiler_params=PARAMS,
    )(edge, body, taps, squares, before)


def part_kernel(k, block, taps, *refs):
    before, outs, acts = refs[:-4], refs[-4:-1], refs[-1]
    parts = [main_taps(block[...], taps, owner_of(k), acts), *edge_taps(block[...], taps, owner_of(k))]
    for place, part in enumerate(parts):
        outs[place][...] = before[place][...] + part if before else part


def second_part(k, block, taps, before):
    cells, width = block.shape
    outs = taps.shape[1]
    return pl.pallas_call(
        lambda *refs: part_kernel(k, *refs),
        out_shape=[jax.ShapeDtypeStruct((size, outs), jnp.float32) for size in (cells, WIDTH, WIDTH)],
        in_specs=[VMEM] * (2 + len(before)),
        out_specs=[VMEM] * 3,
        input_output_aliases={2 + i: i for i in range(len(before))},
        scratch_shapes=[pltpu.VMEM((3, cells + 2 * WIDTH, width), jnp.bfloat16)],
        compiler_params=PARAMS,
    )(block, taps, *before)


def second_edge_kernel(k, edge, taps, above, below, first, second):
    parts = edge_taps(edge[...], taps, owner_of(k))
    first[...], second[...] = to_swap(above[...] + parts[0], below[...] + parts[1])


def second_edge(k, edge, taps, above, below):
    return pl.pallas_call(
        lambda *refs: second_edge_kernel(k, *refs),
        out_shape=[jax.ShapeDtypeStruct(above.shape, above.dtype)] * 2,
        in_specs=[VMEM] * 4,
        out_specs=[VMEM] * 2,
        compiler_params=PARAMS,
    )(edge, taps, above, below)


def second_main_kernel(k, edge, body, taps, before, out, acts):
    block = jnp.concatenate([edge[:WIDTH], body[...], edge[WIDTH:]], axis=0)
    out[...] = before[...] + main_taps(block, taps, owner_of(k), acts)


def second_main(k, edge, body, taps, before):
    return pl.pallas_call(
        lambda *refs: second_main_kernel(k, *refs),
        out_shape=jax.ShapeDtypeStruct(before.shape, before.dtype),
        in_specs=[VMEM] * 4,
        out_specs=VMEM,
        input_output_aliases={3: 0},
        scratch_shapes=[pltpu.VMEM((3, before.shape[0] + 2 * WIDTH, edge.shape[1]), jnp.bfloat16)],
        compiler_params=PARAMS,
    )(edge, body, taps, before)


def to_swap(above, below):
    even = lax.axis_index("rows") % 2 == 0
    return jnp.where(even, below, above), jnp.where(even, above, below)


def joined(main, first, second, bias):
    row = lax.axis_index("rows")
    even, top, low = row % 2 == 0, row == 0, row == lax.axis_size("rows") - 1
    above = jnp.where(even, second[...], first[...])
    below = jnp.where(even, first[...], second[...])
    above, below = jnp.where(top, 0.0, above), jnp.where(low, 0.0, below)
    end = main.shape[0] - WIDTH
    rows = [main[:WIDTH] + above, main[WIDTH:end], main[end:] + below]
    return jnp.concatenate(rows, axis=0) + bias[...]


def middle_kernel(main, first, second, bias, out, squares):
    middle = joined(main, first, second, bias)
    out[...] = middle
    squares[...] = row_of(jnp.sum(middle * middle, axis=1, keepdims=True))


def out_kernel(main, first, second, bias, source, out):
    result = joined(main, first, second, bias).T + source[...].astype(jnp.float32)
    out[...] = result.astype(out.dtype)


def act_kernel(total, values, gain, *refs):
    sums, out = refs[:-1], refs[-1]
    inverse = column_of(1.0 / jnp.sqrt(sum(ref[...] for ref in sums) / total + 1e-6))
    result = silu(values[...] * gain[...] * inverse).astype(out.dtype)
    out[...] = result


def cut_kernel(block, edge, body):
    end = block.shape[0] - WIDTH
    edge[:WIDTH], edge[WIDTH:] = block[:WIDTH], block[end:]
    body[...] = block[WIDTH:end]


def cut(block):
    cells, width = block.shape
    return pl.pallas_call(
        cut_kernel,
        out_shape=[jax.ShapeDtypeStruct((n, width), block.dtype) for n in (2 * WIDTH, cells - 2 * WIDTH)],
        in_specs=[VMEM],
        out_specs=[VMEM] * 2,
        compiler_params=PARAMS,
    )(block)


def act(values, gain, sums, total):
    return pl.pallas_call(
        lambda *refs: act_kernel(total, *refs),
        out_shape=jax.ShapeDtypeStruct(values.shape, jnp.bfloat16),
        in_specs=[VMEM] * (2 + len(sums)),
        out_specs=VMEM,
        compiler_params=PARAMS,
    )(values, gain, *sums)


def with_row_neighbours(sends):
    count = lax.axis_size("rows")
    rounds = []
    for begin, send in enumerate(sends):
        pairs = [(i, (i + 1) % count) for i in range(begin, count, 2)]
        rounds.append(lax.ppermute(send, "rows", pairs + [(b, a) for a, b in pairs]))
    return rounds


def swap(value, step):
    return lax.ppermute(value, "chan", [(i, i ^ step) for i in range(lax.axis_size("chan"))])


def gathered(block, edge, body):
    *steps, last = steps_of(lax.axis_size("chan"))
    blocks = [block] + [swap(block, step) for step in steps]
    return blocks, *[swap(v, last) for v in (edge, body)]


def resident(
    features, gain_first, weight_first, bias_first, gain_second, weight_second, bias_second
):
    channels, frames, cells = features.shape
    total = weight_first.shape[4]
    count = lax.axis_size("chan")
    source = features.reshape(channels, cells)
    taps = fetch(weight_first)
    whole = to_send(source, gain_first.reshape(1, -1))
    blocks, edge, body = gathered(whole, *rest_of(whole))
    sends = first_edge(blocks, edge, taps)
    edges = with_row_neighbours(sends)
    main, squares = first_upper(blocks, edge, taps)
    main = first_main(count - 1, edge, body, taps, squares, main)
    middle, squares = pl.pallas_call(
        middle_kernel,
        out_shape=[
            jax.ShapeDtypeStruct((cells, channels), jnp.float32),
            jax.ShapeDtypeStruct((1, cells), jnp.float32),
        ],
        in_specs=[VMEM] * 4,
        out_specs=[VMEM] * 2,
        compiler_params=PARAMS,
    )(main, *edges, bias_first.reshape(1, -1))
    others = [swap(squares, step) for step in range(count - 1, 0, -1)]
    second = act(middle, gain_second.reshape(1, -1), [squares, *others], total)
    taps = fetch(weight_second)
    blocks, edge, body = gathered(second, *cut(second))
    parts = ()
    for k, block in enumerate(blocks):
        parts = second_part(k, block, taps, parts)
    sends = second_edge(count - 1, edge, taps, *parts[1:])
    edges = with_row_neighbours(sends)
    main = second_main(count - 1, edge, body, taps, parts[0])
    out = pl.pallas_call(
        out_kernel,
        out_shape=jax.ShapeDtypeStruct((channels, cells), features.dtype),
        in_specs=[VMEM] * 5,
        out_specs=VMEM,
        compiler_params=PARAMS,
    )(main, *edges, bias_second.reshape(1, -1), source)
    return out.reshape(channels, frames, cells)


def padded(block, width):
    low = shift_along(block[..., block.shape[-1] - width :], "rows", 1)
    high = shift_along(block[..., :width], "rows", -1)
    return jnp.concatenate([low, block, high], axis=-1)


def activate(values, gain, total):
    mean_sq = lax.psum(jnp.sum(values * values, axis=0, keepdims=True), "chan") / total
    return jax.nn.silu(values * gain[:, None, None] / jnp.sqrt(mean_sq + 1e-06)).astype(jnp.bfloat16)


def convolve(block, kernel):
    whole = padded(lax.all_gather(block, "chan", axis=0, tiled=True), WIDTH)
    channels, frames, cells = whole.shape
    grid = whole.reshape(1, channels, frames, cells // WIDTH, WIDTH)
    result = lax.conv_general_dilated(
        grid,
        kernel,
        (1, 1, 1),
        ((2, 0), (0, 0), (1, 1)),
        dimension_numbers=("NCDHW", "DHWOI", "NCDHW"),
        preferred_element_type=jnp.float32,
    )
    return result[0].reshape(kernel.shape[3], frames, cells - 2 * WIDTH)


def general(features, gain_first, weight_first, bias_first, gain_second, weight_second, bias_second):
    total = weight_first.shape[4]
    source = features.astype(jnp.float32)
    middle = convolve(activate(source, gain_first, total), weight_first) + bias_first[:, None, None]
    result = convolve(activate(middle, gain_second, total), weight_second)
    return (source + result + bias_second[:, None, None]).astype(jnp.bfloat16)


def on_device(
    features, gain_first, weight_first, bias_first, gain_second, weight_second, bias_second
):
    channels, frames, cells = features.shape
    chan, rows = lax.axis_size("chan"), lax.axis_size("rows")
    narrow = channels % LANES or cells < 3 * WIDTH or channels > cells
    if frames != 1 or narrow or chan < 2 or chan & (chan - 1) or rows % 2:
        return general(
            features, gain_first, weight_first, bias_first, gain_second, weight_second, bias_second
        )
    out = resident(
        features, gain_first, weight_first, bias_first, gain_second, weight_second, bias_second
    )
    return out


def solution(mesh):
    in_specs = (
        P("chan", None, "rows"),
        P("chan"),
        P(None, None, None, "chan", None),
        P("chan"),
        P("chan"),
        P(None, None, None, "chan", None),
        P("chan"),
    )
    return jax.shard_map(
        on_device, mesh=mesh, in_specs=in_specs, out_specs=P("chan", None, "rows"), check_vma=False
    )
```
